512 devices in a mesh: wide: 64 (over z, y), narrow: 8 (over x, core).
Axes of the slice: x: 4, y: 8, z: 8, core: 2. Of those that a mesh axis runs over, the one named last changes fastest.
Arguments:
- node_latent: bfloat16 [65536, 512], P(('wide', 'narrow')), may hold values from -6 to 6
- edge_latent: bfloat16 [262144, 512], P(('wide', 'narrow')), may hold values from -6 to 6
- node_cotangent: bfloat16 [65536, 512], P(('wide', 'narrow')), may hold values from -6 to 6
- w_first: bfloat16 [1536, 512], replicated, may hold values from -2 to 2
- bias_first: bfloat16 [512], replicated, may hold values from -4 to 4
- w_second: bfloat16 [512, 512], replicated, may hold values from -2 to 2
- bias_second: bfloat16 [512], replicated, may hold values from -4 to 4
- norm_gain: bfloat16 [512], replicated, may hold values from 0.099609375 to 1.8984375
- send_map: int32 [512, 4, 64], P(('wide', 'narrow')), may hold values from -1 to 127, as said below
- edge_sender: int32 [262144], P(('wide', 'narrow')), may hold values from 0 to 383, as said below
- edge_receiver: int32 [262144], P(('wide', 'narrow')), may hold values from 0 to 127
Outputs:
- node_grad: bfloat16 [65536, 512], P(('wide', 'narrow'))
- edge_grad: bfloat16 [262144, 512], P(('wide', 'narrow'))
- first_update: float32 [1536, 512], P('wide')
- second_update: float32 [512, 512], P('wide')
The draws below stay inside these ranges and needn't reach their ends.
Inputs may be any that keep to these rules, and one draw needn't show every extreme that they name: `send_map`: -1 marks an unused slot; in each row the used slots come first, at most 64, about a third of them on average; in every draw some partition uses all 64 slots toward a wide neighbour; partitions at narrow index 0 send nothing toward block 3 of a lower neighbour and those at the last narrow index nothing toward a higher one. `edge_sender`: a value below 128 is a local node; 128 + k * 64 + s names slot s of received block k, and only slots that the sending partition uses are named.
All inputs are finite; a program needn't handle non-finite values.
Results may differ from the reference program's by a relative error of at most 0.0085.
Values may be sent and summed in bfloat16 or wider, within the bound.
A program may use at most 64 MiB of HBM per device.

```python
import math
import jax
import jax.numpy as jnp
from jax import lax

D = 512
NODE_DEV = 128
EDGE_DEV = 512
HALO = 64
NODES = 65536
EDGES = 262144
N_WIDE = 64
N_NARROW = 8
DEVICES = 512


def halo_counts(key):
    base_key = jax.random.fold_in(key, 101)
    counts = jax.random.randint(jax.random.fold_in(base_key, 1), (DEVICES, 4), 1, 2 * HALO // 3 + 1)
    full_device = jax.random.randint(jax.random.fold_in(base_key, 2), (), 0, DEVICES)
    full_direction = jax.random.randint(jax.random.fold_in(base_key, 3), (), 0, 2)
    row_ids = jnp.arange(DEVICES, dtype=jnp.int32)[:, None]
    col_ids = jnp.arange(4, dtype=jnp.int32)[None, :]
    counts = jnp.where((row_ids == full_device) & (col_ids == full_direction), HALO, counts)
    narrow_index = row_ids % N_NARROW
    counts = jnp.where((col_ids == 2) & (narrow_index == N_NARROW - 1), 0, counts)
    counts = jnp.where((col_ids == 3) & (narrow_index == 0), 0, counts)
    return counts.astype(jnp.int32)


def draw_send_map(key, part):
    counts = halo_counts(key)
    chosen = jax.random.randint(jax.random.fold_in(key, 102), (DEVICES, 4, HALO), 0, NODE_DEV)
    slot_index = jnp.arange(HALO, dtype=jnp.int32)
    return jnp.where(slot_index[None, None, :] < counts[:, :, None], chosen, -1).astype(jnp.int32)


def draw_edge_sender(key, part):
    counts = halo_counts(key).reshape(N_WIDE, N_NARROW, 4)
    zero_col = jnp.zeros_like(counts[:, :1, 0])
    from_lower = jnp.roll(counts[:, :, 0], 1, axis=0)
    from_higher = jnp.roll(counts[:, :, 1], -1, axis=0)
    from_below = jnp.concatenate([zero_col, counts[:, :-1, 2]], 1)
    from_above = jnp.concatenate([counts[:, 1:, 3], zero_col], 1)
    incoming = jnp.stack([from_lower, from_higher, from_below, from_above], -1).reshape(DEVICES, 4)
    device = jnp.arange(EDGES, dtype=jnp.int32) // EDGE_DEV
    kind_draw = jax.random.randint(jax.random.fold_in(key, 103), (EDGES,), 0, 10)
    direction = jax.random.randint(jax.random.fold_in(key, 104), (EDGES,), 0, 4)
    raw_slot = jax.random.randint(jax.random.fold_in(key, 105), (EDGES,), 0, 1 << 20)
    local_ids = jax.random.randint(jax.random.fold_in(key, 106), (EDGES,), 0, NODE_DEV)
    live_count = incoming[device, direction]
    remote = NODE_DEV + direction * HALO + raw_slot % jnp.maximum(live_count, 1)
    use_remote = (kind_draw < 4) & (live_count > 0)
    return jnp.where(use_remote, remote, local_ids).astype(jnp.int32)


def scaled_weight(key, row_count, col_count):
    base_draw = jnp.clip(jax.random.normal(jax.random.fold_in(key, 1), (row_count, col_count), jnp.float32), -3.0, 3.0)
    row_scale = jnp.exp(jax.random.uniform(jax.random.fold_in(key, 2), (row_count, 1), jnp.float32, math.log(0.3), math.log(3.0)))
    col_scale = jnp.exp(jax.random.uniform(jax.random.fold_in(key, 3), (1, col_count), jnp.float32, math.log(0.3), math.log(3.0)))
    return (base_draw * row_scale * col_scale / (1.39 * math.sqrt(row_count))).astype(jnp.bfloat16)


def draw_w_first(key, part):
    return scaled_weight(jax.random.fold_in(key, 21), 3 * D, D)


def draw_w_second(key, part):
    return scaled_weight(jax.random.fold_in(key, 22), D, D)


def place_ends(array, stream_key, low, top_value):
    longest = array.shape.index(max(array.shape))
    spots = []
    for shift in (0, 1):
        where = [jax.random.randint(jax.random.fold_in(stream_key, axis), (), 0, length) for axis, length in enumerate(array.shape)]
        where[longest] = (where[longest] + shift) % array.shape[longest]
        spots.append(tuple(where))
    return array.at[spots[0]].set(low).at[spots[1]].set(top_value)


def steps_of(own_key, extent, shards, low, top_value):
    loudness, own = 1.0, jax.random.fold_in(own_key, 6)
    for position, parts in shards:
        heights = jnp.exp(jax.random.uniform(jax.random.fold_in(own, position), (parts,), jnp.float32, low / len(shards), top_value / len(shards)))
        loudness = loudness * jnp.repeat(heights, extent[position] // parts).reshape([-1 if axis == position else 1 for axis in range(len(extent))])
    return loudness


def normal_values(stream_key, shape, spread, bound, cuts=(), kind=jnp.bfloat16):
    entries = spread * jax.random.normal(stream_key, shape, jnp.float32)
    if cuts:
        entries = entries * steps_of(stream_key, shape, cuts, -0.22, 0.18)
    return jnp.clip(entries, -bound, bound).astype(kind)


def setup_inputs(seed: int = 0) -> dict:
    key_of = jax.random.split(jax.random.key(seed), 12)
    node_latent = normal_values(key_of[0], (NODES, D), 1.0, 6.0, ((0, 512),))
    edge_latent = normal_values(key_of[1], (EDGES, D), 1.0, 6.0, ((0, 512),))
    node_cotangent = normal_values(key_of[2], (NODES, D), 1.0, 6.0, ((0, 512),))
    w_first = draw_w_first(jax.random.fold_in(key_of[11], 71), 0)
    bias_first = normal_values(key_of[4], (D,), 1.0, 4.0)
    w_second = draw_w_second(jax.random.fold_in(key_of[11], 71), 0)
    bias_second = normal_values(key_of[6], (D,), 1.0, 4.0)
    norm_gain = jnp.clip(1.0 + 0.18 * jax.random.normal(key_of[7], (D,), jnp.float32), 0.099609375, 1.8984375).astype(jnp.bfloat16)
    send_map = draw_send_map(jax.random.fold_in(key_of[11], 71), 0)
    edge_sender = draw_edge_sender(jax.random.fold_in(key_of[11], 71), 0)
    edge_receiver = place_ends(jax.random.randint(key_of[10], (EDGES,), 0, NODE_DEV), jax.random.fold_in(key_of[10], 1), 0, NODE_DEV - 1).astype(jnp.int32)
    return dict(node_latent=node_latent, edge_latent=edge_latent, node_cotangent=node_cotangent, w_first=w_first, bias_first=bias_first, w_second=w_second, bias_second=bias_second, norm_gain=norm_gain, send_map=send_map, edge_sender=edge_sender, edge_receiver=edge_receiver)


def narrow_shift(blocks, direction):
    zero_col = jnp.zeros_like(blocks[:, :1])
    if direction == 1:
        return jnp.concatenate([zero_col, blocks[:, :-1]], 1)
    return jnp.concatenate([blocks[:, 1:], zero_col], 1)

def norm_parts(second_pre):
    mean_value = lax.optimization_barrier(jnp.mean(second_pre, -1, keepdims=True))
    centered = second_pre - mean_value
    variance = lax.optimization_barrier(jnp.mean(centered * centered, -1, keepdims=True))
    inv_std = lax.rsqrt(variance + 1e-05)
    return (centered * inv_std, inv_std)

def edge_terms(node_table, own_nodes, own_cot, own_edges, sender_ids, receiver_ids, w_first, bias_first, w_second, bias_second, norm_gain):
    feature_width = own_edges.shape[1]
    sender_rows = node_table[sender_ids]
    receiver_rows = own_nodes[receiver_ids]
    inputs = jnp.concatenate([own_edges, sender_rows, receiver_rows], 1)
    preact = jnp.dot(inputs, w_first, preferred_element_type=jnp.float32) + bias_first.astype(jnp.float32)
    activation = jax.nn.silu(preact).astype(jnp.bfloat16)
    second_pre = jnp.dot(activation, w_second, preferred_element_type=jnp.float32) + bias_second.astype(jnp.float32)
    normalized, inv_std = norm_parts(second_pre)
    upstream = own_cot[receiver_ids].astype(jnp.float32)
    scaled = upstream * norm_gain.astype(jnp.float32)
    norm_back = (inv_std * (scaled - lax.optimization_barrier(jnp.mean(scaled, -1, keepdims=True)) - normalized * lax.optimization_barrier(jnp.mean(scaled * normalized, -1, keepdims=True)))).astype(jnp.bfloat16)
    second_grad = jnp.dot(activation.T, norm_back, preferred_element_type=jnp.float32)
    sigmoid_pre = jax.nn.sigmoid(preact)
    pre_back = (jnp.dot(norm_back, w_second.T, preferred_element_type=jnp.float32) * sigmoid_pre * (1.0 + preact * (1.0 - sigmoid_pre))).astype(jnp.bfloat16)
    first_grad = jnp.dot(inputs.T, pre_back, preferred_element_type=jnp.float32)
    input_back = jnp.dot(pre_back, w_first.T, preferred_element_type=jnp.float32)
    edge_grad = (upstream + input_back[:, :feature_width]).astype(jnp.bfloat16)
    table_grad = jax.ops.segment_sum(input_back[:, feature_width:2 * feature_width], sender_ids, num_segments=node_table.shape[0])
    receiver_grad = jax.ops.segment_sum(input_back[:, 2 * feature_width:], receiver_ids, num_segments=own_nodes.shape[0])
    return (edge_grad, table_grad, receiver_grad, first_grad, second_grad)

def clip_update(grad_total, weight):
    row_count = grad_total.shape[0]
    grad_sq = lax.optimization_barrier(jnp.sum(grad_total * grad_total, 0))
    weight_sq = lax.optimization_barrier(jnp.sum(jnp.square(weight.astype(jnp.float32)), 0))
    unit_ratio = jnp.sqrt((grad_sq + 1e-06) / (weight_sq + 1e-06))
    mean_ratio = jnp.mean(unit_ratio)
    factor = jnp.minimum(1.0 / (mean_ratio * jnp.sqrt(weight_sq + 1e-06)), 1.0 / jnp.sqrt(grad_sq + 1e-06))
    return grad_total * factor * math.sqrt(row_count)

def reference(node_latent, edge_latent, node_cotangent, w_first, bias_first, w_second, bias_second, norm_gain, send_map, edge_sender, edge_receiver):
    node_blocks = node_latent.reshape(N_WIDE, N_NARROW, NODE_DEV, D)
    slot_map = send_map.reshape(N_WIDE, N_NARROW, 4, HALO)
    live_slot = slot_map >= 0
    safe_map = jnp.where(live_slot, slot_map, 0).astype(jnp.int32)
    wide_ids = jnp.arange(N_WIDE, dtype=jnp.int32)[:, None, None, None]
    narrow_ids = jnp.arange(N_NARROW, dtype=jnp.int32)[None, :, None, None]
    outgoing = node_blocks[wide_ids, narrow_ids, safe_map]
    outgoing = jnp.where(live_slot[..., None], outgoing, jnp.zeros_like(outgoing))
    received = jnp.stack([jnp.roll(outgoing[:, :, 0], 1, axis=0), jnp.roll(outgoing[:, :, 1], -1, axis=0), narrow_shift(outgoing[:, :, 2], 1), narrow_shift(outgoing[:, :, 3], -1)], 2)
    node_table = jnp.concatenate([node_blocks, received.reshape(N_WIDE, N_NARROW, 4 * HALO, D)], 2)
    cot_blocks = node_cotangent.reshape(N_WIDE, N_NARROW, NODE_DEV, D)
    edge_blocks = edge_latent.reshape(N_WIDE, N_NARROW, EDGE_DEV, D)
    sender_blocks = edge_sender.reshape(N_WIDE, N_NARROW, EDGE_DEV)
    receiver_blocks = edge_receiver.reshape(N_WIDE, N_NARROW, EDGE_DEV)

    def device_terms(table_part, node_part, cot_part, edge_part, sender_part, receiver_part):
        return edge_terms(table_part, node_part, cot_part, edge_part, sender_part, receiver_part, w_first, bias_first, w_second, bias_second, norm_gain)

    def edge_block(totals, block_data):
        edge_grad, table_grad, receiver_grad, first_grad, second_grad = jax.vmap(device_terms)(*block_data)
        totals = (totals[0] + lax.optimization_barrier(jnp.sum(first_grad, 0)), totals[1] + lax.optimization_barrier(jnp.sum(second_grad, 0)))
        return (totals, (edge_grad, table_grad, receiver_grad))
    initial = (jnp.zeros((3 * D, D), jnp.float32), jnp.zeros((D, D), jnp.float32))
    totals, outputs = lax.scan(edge_block, initial, (node_table, node_blocks, cot_blocks, edge_blocks, sender_blocks, receiver_blocks))
    edge_grads, table_grads, receiver_grads = outputs
    halo_grad = table_grads[:, :, NODE_DEV:].reshape(N_WIDE, N_NARROW, 4, HALO, D).astype(jnp.bfloat16)
    returned = jnp.stack([jnp.roll(halo_grad[:, :, 0], -1, axis=0), jnp.roll(halo_grad[:, :, 1], 1, axis=0), narrow_shift(halo_grad[:, :, 2], -1), narrow_shift(halo_grad[:, :, 3], 1)], 2)
    send_hot = (slot_map[..., None] == jnp.arange(NODE_DEV, dtype=jnp.int32)).astype(jnp.float32)
    back = jnp.einsum('abkhn,abkhd->abnd', send_hot, returned.astype(jnp.float32), precision=lax.Precision.HIGHEST)
    node_grad = (cot_blocks.astype(jnp.float32) + table_grads[:, :, :NODE_DEV] + receiver_grads + back).astype(jnp.bfloat16)
    first_update = clip_update(totals[0], w_first)
    second_update = clip_update(totals[1], w_second)
    return (node_grad.reshape(NODES, D), edge_grads.reshape(EDGES, D), first_update, second_update)
```

```python
import math

import jax
import jax.numpy as jnp
from jax import lax
from jax.sharding import Mesh
from jax.experimental import pallas as pl
from jax.experimental.pallas import tpu as pltpu
from jax.sharding import PartitionSpec as P

WIDE = ("z", "y")
NARROW = ("x", "c")
WIDE_NARROW = ("z", "y", "x", "c")


def shifted(value, axis, steps):
    count = lax.axis_size(axis)
    pairs = [(source, (source + steps) % count) for source in range(count)]
    return lax.ppermute(value, axis, pairs)


def shifted_2(block, axis, distance):
    devices = range(lax.axis_size(axis))
    route = [(i - distance, i) for i in devices if i - distance in devices]
    return lax.ppermute(block, axis, route)


def neighbours(blocks, direction):
    higher = shifted(blocks[0], WIDE, direction)
    lower = shifted(blocks[1], WIDE, -direction)
    up_side = shifted_2(blocks[2], NARROW, direction)
    down_side = shifted_2(blocks[3], NARROW, -direction)
    return jnp.stack([higher, lower, up_side, down_side], 0)


def norm_parts(second_pre):
    mean_value = jnp.mean(second_pre, -1, keepdims=True)
    centered = second_pre - mean_value
    variance = jnp.mean(centered * centered, -1, keepdims=True)
    inv_std = lax.rsqrt(variance + 1e-05)
    return (centered * inv_std, inv_std)


def edge_contract(hot_table, values):
    return lax.dot_general(
        hot_table,
        values,
        (((0,), (0,)), ((), ())),
        precision=lax.Precision.HIGHEST,
        preferred_element_type=jnp.float32,
    )


MESH = pl.DeviceIdType.MESH
F32 = jnp.float32
BF16 = jnp.bfloat16


class Comm:
    def __init__(self, send_sems, recv_sems):
        self.send_sems, self.recv_sems, self.used, self.started = send_sems, recv_sems, 0, []

    def copy(self, src, dst, to):
        copy = pltpu.make_async_remote_copy(
            src_ref=src,
            dst_ref=dst,
            send_sem=self.send_sems.at[self.used],
            recv_sem=self.recv_sems.at[self.used],
            device_id=to,
            device_id_type=MESH,
        )
        self.used += 1
        self.started.append(copy)
        copy.start()
        return copy

    def drain(self):
        for copy in self.started:
            copy.wait_send()


class Ring:
    def __init__(self, comm, axis, total, slots):
        self.comm, self.axis, self.total = comm, axis, total
        self.count, self.me = lax.axis_size(axis), lax.axis_index(axis)
        self.half = total.shape[1] // 2
        self.chains = []
        used = 0
        for half in (0, 1):
            for sign in (-1, 1):
                hops = self.count // 2 - (0 if (sign < 0) == (half == 0) else 1)
                self.chains.append((half, sign, hops, slots.at[pl.ds(used, max(hops, 1))]))
                used += hops
        self.last = [None] * 4

    def part(self, owner, half):
        return self.total.at[owner, pl.ds(half * self.half, self.half)]

    def step(self, step):
        for i, (half, sign, hops, slots) in enumerate(self.chains):
            if step >= hops:
                continue
            owner = lax.rem(self.me + sign * (hops - step) + self.count, self.count)
            mine = self.part(owner, half)
            if step:
                self.last[i].wait_recv()
                mine[...] = (mine[...].astype(F32) + slots[step - 1].astype(F32)).astype(BF16)
            to = lax.rem(self.me + sign + self.count, self.count)
            self.last[i] = self.comm.copy(mine, slots.at[step], {self.axis: to})

    def finish(self, out):
        for half in (0, 1):
            here = self.part(self.me, half)
            value = here[...].astype(F32)
            for i, (chain_half, _, hops, slots) in enumerate(self.chains):
                if chain_half == half and hops:
                    self.last[i].wait_recv()
                    value = value + slots[hops - 1].astype(F32)
            out[pl.ds(half * self.half, self.half)] = value.astype(BF16)


def scatter(comm, axis, parts, slots):
    count, me = lax.axis_size(axis), lax.axis_index(axis)
    copies = []
    for k in range(1, count):
        peer = lax.rem(me + k, count)
        copies.append(comm.copy(parts(peer), slots.at[k - 1], {axis: peer}))
    return copies


def entry_barrier():
    barrier = pltpu.get_barrier_semaphore()
    signals = 0
    for axis in ("z", "y"):
        count, me = lax.axis_size(axis), lax.axis_index(axis)
        for k in range(1, count):
            pl.semaphore_signal(barrier, 1, device_id={axis: lax.rem(me + k, count)}, device_id_type=MESH)
            signals += 1
    for device in others_nearby():
        pl.semaphore_signal(barrier, 1, device_id=device[1], device_id_type=MESH)
        signals += 1
    pl.semaphore_wait(barrier, signals)


def others_nearby():
    across, cores = lax.axis_size("x"), lax.axis_size("c")
    x, c = lax.axis_index("x"), lax.axis_index("c")
    found = []
    for k in range(1, across * cores):
        to_x, to_c = lax.rem(x + k // cores, across), lax.rem(c + k % cores, cores)
        found.append((k, {"x": to_x, "c": to_c}))
    return found


def clip_rows(grad_sq, weight_sq, which):
    ratio = jnp.sqrt((grad_sq + 1e-06) / (weight_sq + 1e-06))
    rows = lax.broadcasted_iota(jnp.int32, ratio.shape, 0)
    mine = lax.rem(rows, 2) == which
    mean_ratio = jnp.sum(jnp.where(mine, ratio, 0.0)) / (ratio.shape[0] // 2 * ratio.shape[1])
    return jnp.minimum(1.0 / (mean_ratio * jnp.sqrt(weight_sq + 1e-06)), 1.0 / jnp.sqrt(grad_sq + 1e-06))


def reduce_kernel(
    grads_a,
    grads_b,
    weight_sq,
    first_out,
    second_out,
    from_core_a,
    from_core_b,
    total_a,
    total_b,
    ring_a,
    ring_b,
    over_a,
    over_b,
    cross_a,
    cross_b,
    share,
    shares,
    squares,
    squares_in,
    send_sems,
    recv_sems,
):
    comm = Comm(send_sems, recv_sems)
    c = lax.axis_index("c")
    nz, ny, across = lax.axis_size("z"), lax.axis_size("y"), lax.axis_size("x")
    entry_barrier()
    other = 1 - c
    pair_a = comm.copy(grads_a.at[other], from_core_a, {"c": other})
    pair_b = comm.copy(grads_b.at[other], from_core_b, {"c": other})
    for pair, grads, arrived, total in (
        (pair_a, grads_a, from_core_a, total_a),
        (pair_b, grads_b, from_core_b, total_b),
    ):
        pair.wait_recv()

        def add(i, _, grads=grads, arrived=arrived, total=total):
            total[i] = (grads[c, i].astype(F32) + arrived[i].astype(F32)).astype(BF16)
            return 0

        lax.fori_loop(0, total.shape[0], add, 0)
    rings = (Ring(comm, "y", total_a, ring_a), Ring(comm, "z", total_b, ring_b))
    for step in range(max(nz, ny) // 2):
        for ring in rings:
            ring.step(step)
    rings[0].finish(over_a)
    to_z = scatter(comm, "z", lambda peer: over_a.at[peer], cross_a)
    rings[1].finish(over_b)
    to_y = scatter(comm, "y", lambda peer: over_b.at[peer], cross_b)
    for i, (axis, copies, over, cross) in enumerate(
        (("z", to_z, over_a, cross_a), ("y", to_y, over_b, cross_b))
    ):
        value = over[lax.axis_index(axis)].astype(F32)
        for k, copy in enumerate(copies):
            copy.wait_recv()
            value = value + cross[k].astype(F32)
        share[i] = value.astype(BF16)
    here = lax.axis_index("x") * 2 + c
    shares[here] = share[...]
    copies = [comm.copy(share, shares.at[here], device) for _, device in others_nearby()]
    for copy in copies:
        copy.wait_recv()
    slabs = []
    for core in (0, 1):
        for i in (0, 1):
            value = shares[core, i].astype(F32)
            for x in range(1, across):
                value = value + shares[2 * x + core, i].astype(F32)
            slabs.append(value)
    first_rows = first_out.shape[0]
    sums = []
    for value in slabs:
        square = value * value
        sums.append(jnp.sum(square[:first_rows], 0, keepdims=True))
        sums.append(jnp.sum(square[first_rows:], 0, keepdims=True))
    squares[0] = jnp.concatenate(sums, 0)
    copies = scatter(comm, "y", lambda peer: squares.at[0], squares_in.at[pl.ds(0, ny - 1)])
    value = squares[0]
    for k, copy in enumerate(copies):
        copy.wait_recv()
        value = value + squares_in[k]
    squares[1] = value
    copies = scatter(comm, "z", lambda peer: squares.at[1], squares_in.at[pl.ds(ny - 1, nz - 1)])
    for k, copy in enumerate(copies):
        copy.wait_recv()
        value = value + squares_in[ny - 1 + k]
    factors = [clip_rows(value, weight_sq[...], which) for which in (0, 1)]
    for i, slab in enumerate(slabs):
        columns = pl.ds(128 * i, 128)
        first = factors[0][2 * i : 2 * i + 1] * math.sqrt(first_rows * nz * ny)
        second = factors[1][2 * i + 1 : 2 * i + 2] * math.sqrt(second_out.shape[0] * nz * ny)
        first_out[:, columns] = slab[:first_rows] * first
        second_out[:, columns] = slab[first_rows:] * second
    comm.drain()


def reduce_updates(first_grad, second_grad, w_first, w_second):
    nz, ny, across = lax.axis_size("z"), lax.axis_size("y"), lax.axis_size("x")
    shards = nz * ny
    rows = (first_grad.shape[0] + second_grad.shape[0]) // shards
    first_rows, second_rows = first_grad.shape[0] // shards, second_grad.shape[0] // shards
    blocks = jnp.concatenate(
        [
            first_grad.astype(BF16).reshape(nz, ny, first_rows, 2, 2, 128),
            second_grad.astype(BF16).reshape(nz, ny, second_rows, 2, 2, 128),
        ],
        2,
    )
    grads_a = jnp.transpose(blocks[:, :, :, :, 0], (3, 1, 0, 2, 4))
    grads_b = jnp.transpose(blocks[:, :, :, :, 1], (3, 0, 1, 2, 4))
    weight_sq = jnp.stack(
        [
            jnp.sum(jnp.square(w_first.astype(F32)), 0).reshape(4, 128),
            jnp.sum(jnp.square(w_second.astype(F32)), 0).reshape(4, 128),
        ],
        1,
    ).reshape(8, 128)
    vmem = pl.BlockSpec(memory_space=pltpu.VMEM)
    copies = 2 + 2 * 2 * (ny - 1 + nz - 1) + 2 * (nz - 1 + ny - 1) + 2 * across - 1
    return pl.pallas_call(
        reduce_kernel,
        out_shape=(
            jax.ShapeDtypeStruct((first_rows, 512), F32),
            jax.ShapeDtypeStruct((second_rows, 512), F32),
        ),
        in_specs=[vmem] * 3,
        out_specs=(vmem, vmem),
        scratch_shapes=[
            pltpu.VMEM((ny, nz, rows, 128), BF16),
            pltpu.VMEM((nz, ny, rows, 128), BF16),
            pltpu.VMEM((ny, nz, rows, 128), BF16),
            pltpu.VMEM((nz, ny, rows, 128), BF16),
            pltpu.VMEM((2 * (ny - 1), nz // 2, rows, 128), BF16),
            pltpu.VMEM((2 * (nz - 1), ny // 2, rows, 128), BF16),
            pltpu.VMEM((nz, rows, 128), BF16),
            pltpu.VMEM((ny, rows, 128), BF16),
            pltpu.VMEM((nz - 1, rows, 128), BF16),
            pltpu.VMEM((ny - 1, rows, 128), BF16),
            pltpu.VMEM((2, rows, 128), BF16),
            pltpu.VMEM((2 * across, 2, rows, 128), BF16),
            pltpu.VMEM((2, 8, 128), F32),
            pltpu.VMEM((ny - 1 + nz - 1, 8, 128), F32),
            pltpu.SemaphoreType.DMA((copies,)),
            pltpu.SemaphoreType.DMA((copies,)),
        ],
        compiler_params=pltpu.CompilerParams(collective_id=0, has_side_effects=True, vmem_limit_bytes=32 << 20),
    )(grads_a, grads_b, weight_sq)


def per_device(
    node_latent,
    edge_latent,
    node_cotangent,
    w_first,
    bias_first,
    w_second,
    bias_second,
    norm_gain,
    send_map,
    edge_sender,
    edge_receiver,
):
    node_count, feature_width = node_latent.shape
    halo_slots = send_map.shape[2]
    table_rows = node_count + 4 * halo_slots
    send_hot = (send_map[0][:, :, None] == jnp.arange(node_count, dtype=jnp.int32)).astype(
        jnp.bfloat16
    )
    outgoing = jnp.einsum(
        "khn,nd->khd", send_hot, node_latent, preferred_element_type=jnp.float32
    ).astype(jnp.bfloat16)
    received = neighbours(outgoing, 1)
    node_table = jnp.concatenate([node_latent, received.reshape(4 * halo_slots, feature_width)], 0)
    sender_hot = (edge_sender[:, None] == jnp.arange(table_rows, dtype=jnp.int32)).astype(
        jnp.bfloat16
    )
    receiver_hot = (edge_receiver[:, None] == jnp.arange(node_count, dtype=jnp.int32)).astype(
        jnp.bfloat16
    )
    sender_rows = jnp.dot(sender_hot, node_table, preferred_element_type=jnp.float32).astype(
        jnp.bfloat16
    )
    receiver_rows = jnp.dot(receiver_hot, node_latent, preferred_element_type=jnp.float32).astype(
        jnp.bfloat16
    )
    inputs = jnp.concatenate([edge_latent, sender_rows, receiver_rows], 1)
    preact = jnp.dot(inputs, w_first, preferred_element_type=jnp.float32) + bias_first.astype(
        jnp.float32
    )
    activation = jax.nn.silu(preact).astype(jnp.bfloat16)
    second_pre = jnp.dot(
        activation, w_second, preferred_element_type=jnp.float32
    ) + bias_second.astype(jnp.float32)
    normalized, inv_std = norm_parts(second_pre)
    upstream = jnp.dot(receiver_hot, node_cotangent, preferred_element_type=jnp.float32)
    scaled = upstream * norm_gain.astype(jnp.float32)
    norm_back = (
        inv_std
        * (
            scaled
            - jnp.mean(scaled, -1, keepdims=True)
            - normalized * jnp.mean(scaled * normalized, -1, keepdims=True)
        )
    ).astype(jnp.bfloat16)
    second_grad = lax.dot_general(
        activation, norm_back, (((0,), (0,)), ((), ())), preferred_element_type=jnp.float32
    )
    sigmoid_pre = jax.nn.sigmoid(preact)
    pre_back = (
        jnp.dot(norm_back, w_second.T, preferred_element_type=jnp.float32)
        * sigmoid_pre
        * (1.0 + preact * (1.0 - sigmoid_pre))
    ).astype(jnp.bfloat16)
    first_grad = lax.dot_general(
        inputs, pre_back, (((0,), (0,)), ((), ())), preferred_element_type=jnp.float32
    )
    input_back = jnp.dot(pre_back, w_first.T, preferred_element_type=jnp.float32)
    edge_grad = (upstream + input_back[:, :feature_width]).astype(jnp.bfloat16)
    table_grad = edge_contract(
        sender_hot.astype(jnp.float32), input_back[:, feature_width : 2 * feature_width]
    )
    receiver_grad = edge_contract(
        receiver_hot.astype(jnp.float32), input_back[:, 2 * feature_width :]
    )
    halo_grad = table_grad[node_count:].reshape(4, halo_slots, feature_width).astype(jnp.bfloat16)
    returned = neighbours(halo_grad, -1)
    back = jnp.einsum("khn,khd->nd", send_hot, returned, preferred_element_type=jnp.float32)
    node_grad = (
        node_cotangent.astype(jnp.float32) + table_grad[:node_count] + receiver_grad + back
    ).astype(jnp.bfloat16)
    first_update, second_update = reduce_updates(first_grad, second_grad, w_first, w_second)
    return (node_grad, edge_grad, first_update, second_update)


def solution(mesh):
    finer = Mesh(mesh.devices.reshape(8, 8, 4, 2), WIDE_NARROW)
    in_specs = (
        P(WIDE_NARROW, None),
        P(WIDE_NARROW, None),
        P(WIDE_NARROW, None),
        P(),
        P(),
        P(),
        P(),
        P(),
        P(WIDE_NARROW, None, None),
        P(WIDE_NARROW),
        P(WIDE_NARROW),
    )
    out_specs = (P(WIDE_NARROW, None), P(WIDE_NARROW, None), P(WIDE, None), P(WIDE, None))
    return jax.shard_map(
        per_device, mesh=finer, in_specs=in_specs, out_specs=out_specs, check_vma=False
    )
```

```python
import math

import jax
import jax.numpy as jnp
from jax import lax
from jax.experimental import pallas as pl
from jax.experimental.pallas import tpu as pltpu
from jax.sharding import Mesh
from jax.sharding import PartitionSpec as P

WIDE = ("z", "y")
ALL = ("z", "y", "x", "c")
MESH = pl.DeviceIdType.MESH
F32 = jnp.float32
BF16 = jnp.bfloat16
ROWS = 256


def dot(a, b):
    return jnp.dot(a, b, preferred_element_type=F32)


def dot_nt(a, b):
    return lax.dot_general(a, b, (((1,), (1,)), ((), ())), preferred_element_type=F32)


class Comm:
    def __init__(self, send_sems, recv_sems):
        self.send_sems, self.recv_sems, self.used, self.started = send_sems, recv_sems, 0, []

    def copy(self, src, dst, to):
        copy = pltpu.make_async_remote_copy(
            src_ref=src,
            dst_ref=dst,
            send_sem=self.send_sems.at[self.used],
            recv_sem=self.recv_sems.at[self.used],
            device_id=to,
            device_id_type=MESH,
        )
        self.used += 1
        self.started.append(copy)
        copy.start()
        return copy

    def drain(self):
        for copy in self.started:
            copy.wait_send()


class Ring:
    def __init__(self, comm, axis, own, paired, staged, slots):
        self.comm, self.axis, self.own, self.paired = comm, axis, own, paired
        self.count, self.me = lax.axis_size(axis), lax.axis_index(axis)
        self.half = own.shape[1] // 2
        self.chains = []
        used = 0
        for half in (0, 1):
            for sign in (-1, 1):
                hops = self.count // 2 - (0 if (sign < 0) == (half == 0) else 1)
                span = pl.ds(used, max(hops, 1))
                self.chains.append((half, sign, hops, staged.at[span], slots.at[span]))
                used += hops
        self.last = [None] * 4

    def value(self, owner, half):
        part = pl.ds(half * self.half, self.half)
        return self.own[owner, part] + self.paired[owner, part].astype(F32)

    def step(self, step):
        for i, (half, sign, hops, staged, slots) in enumerate(self.chains):
            if step >= hops:
                continue
            owner = lax.rem(self.me + sign * (hops - step) + self.count, self.count)
            value = self.value(owner, half)
            if step:
                self.last[i].wait_recv()
                value = value + slots[step - 1].astype(F32)
            staged[step] = value.astype(BF16)
            to = lax.rem(self.me + sign + self.count, self.count)
            self.last[i] = self.comm.copy(staged.at[step], slots.at[step], {self.axis: to})

    def finish(self, over, over_sent):
        for half in (0, 1):
            value = self.value(self.me, half)
            for i, (chain_half, _, hops, _, slots) in enumerate(self.chains):
                if chain_half == half and hops:
                    self.last[i].wait_recv()
                    value = value + slots[hops - 1].astype(F32)
            part = pl.ds(half * self.half, self.half)
            over[part] = value
            over_sent[part] = value.astype(BF16)


def offsets(count):
    return sorted(range(1, count), key=lambda k: -min(k, count - k))


def scatter(comm, axis, parts, slots):
    count, me = lax.axis_size(axis), lax.axis_index(axis)
    copies = []
    for k in offsets(count):
        peer = lax.rem(me + k, count)
        copies.append(comm.copy(parts(peer), slots.at[k - 1], {axis: peer}))
    return copies


def total_of(copies, own, slots):
    value = own
    for copy in copies:
        copy.wait_recv()
    for k in range(len(copies)):
        value = value + slots[k].astype(F32)
    return value


def narrow_peers():
    across, cores = lax.axis_size("x"), lax.axis_size("c")
    x, c = lax.axis_index("x"), lax.axis_index("c")
    steps = offsets(across) + [0]
    return [
        {"x": lax.rem(x + i, across), "c": lax.rem(c + j, cores)}
        for i in steps
        for j in range(cores)
        if i or j
    ]


def wide_neighbour(step):
    nz, ny = lax.axis_size("z"), lax.axis_size("y")
    index = lax.rem(lax.axis_index("z") * ny + lax.axis_index("y") + step + nz * ny, nz * ny)
    return {"z": index // ny, "y": lax.rem(index, ny)}


def narrow_neighbour(step):
    across, cores = lax.axis_size("x"), lax.axis_size("c")
    count = across * cores
    index = lax.rem(lax.axis_index("x") * cores + lax.axis_index("c") + step + count, count)
    return {"x": index // cores, "c": lax.rem(index, cores)}


def greeted():
    found = [wide_neighbour(1), wide_neighbour(-1)]
    for axis in ("z", "y"):
        count, me = lax.axis_size(axis), lax.axis_index(axis)
        found += [{axis: lax.rem(me + k, count)} for k in offsets(count)]
    return found + narrow_peers()


def as_columns(row):
    blocks = [
        jnp.transpose(jnp.broadcast_to(row[:, 128 * i : 128 * (i + 1)], (128, 128)))
        for i in range(row.shape[1] // 128)
    ]
    return jnp.concatenate(blocks, 0)


def hot_rows(row, count):
    ids = lax.broadcasted_iota(jnp.int32, (count, row.shape[1]), 0)
    return jnp.where(ids == row, 1.0, 0.0).astype(BF16)


def hot_columns(row, count):
    columns = as_columns(row)
    ids = lax.broadcasted_iota(jnp.int32, columns.shape, 1)
    blocks = [jnp.where(columns == ids + 128 * i, 1.0, 0.0) for i in range(count // 128)]
    return jnp.concatenate(blocks, 1).astype(BF16)


def clip_rows(grad_sq, weight_sq, which):
    ratio = jnp.sqrt((grad_sq + 1e-06) / (weight_sq + 1e-06))
    rows = lax.broadcasted_iota(jnp.int32, ratio.shape, 0)
    mine = lax.rem(rows, 2) == which
    mean_ratio = jnp.sum(jnp.where(mine, ratio, 0.0)) / (ratio.shape[0] // 2 * ratio.shape[1])
    return jnp.minimum(1.0 / (mean_ratio * jnp.sqrt(weight_sq + 1e-06)), 1.0 / jnp.sqrt(grad_sq + 1e-06))


def slab_rows(first, second):
    rows = []
    for i in range(4):
        columns = slice(128 * i, 128 * (i + 1))
        rows += [
            jnp.sum(first[:, columns], 0, keepdims=True),
            jnp.sum(second[:, columns], 0, keepdims=True),
        ]
    return jnp.concatenate(rows, 0)


def split_blocks(value, out_a, out_b, rows):
    ny, nz = out_a.shape[:2]
    height = value.shape[0] // (ny * nz)
    lower = value[:, :128].reshape(nz, ny, height, 128)
    for y in range(ny):
        out_a[y, :, rows, :] = lower[:, y].astype(out_a.dtype)
    out_b[:, :, rows, :] = value[:, 128:].reshape(nz, ny, height, 128).astype(out_b.dtype)


def kernel(
    ids,
    vectors,
    node_hbm,
    edge_hbm,
    cot_hbm,
    w_first_hbm,
    w_second_hbm,
    node_grad_out,
    edge_grad_out,
    first_out,
    second_out,
    table,
    edge,
    cot,
    w_first,
    w_second,
    outgoing,
    inputs_t,
    preact,
    upstream,
    activation_t,
    norm_back,
    pre_back,
    from_sender,
    weight_sq,
    halo_grad,
    returned,
    local_grad,
    sent_a,
    sent_b,
    from_core_a,
    from_core_b,
    own_a,
    own_b,
    staged_a,
    staged_b,
    ring_a,
    ring_b,
    over_a,
    over_b,
    over_sent_a,
    over_sent_b,
    cross_a,
    cross_b,
    share,
    shares,
    squares,
    squares_in,
    load_sems,
    send_sems,
    recv_sems,
):
    comm = Comm(send_sems, recv_sems)
    c = lax.axis_index("c")
    nz, ny, across = lax.axis_size("z"), lax.axis_size("y"), lax.axis_size("x")
    nodes, width = node_hbm.shape
    edges = edge_hbm.shape[0]
    slots = outgoing.shape[1]
    barrier = pltpu.get_barrier_semaphore()
    peers = greeted()
    for peer in peers:
        pl.semaphore_signal(barrier, 1, device_id=peer, device_id_type=MESH)
    loads = [
        pltpu.make_async_copy(src, dst, load_sems.at[i])
        for i, (src, dst) in enumerate(
            (
                (node_hbm, table.at[pl.ds(0, nodes)]),
                (edge_hbm, edge),
                (w_first_hbm, w_first),
                (cot_hbm, cot),
                (w_second_hbm, w_second),
            )
        )
    ]
    for load in loads:
        load.start()
    send_row = ids[:, : 4 * slots]
    sender_row = ids[:, 4 * slots : 4 * slots + edges]
    receiver_row = ids[:, 4 * slots + edges :]
    send_hot = hot_columns(send_row, nodes)
    receiver_hot = hot_columns(receiver_row, nodes)
    loads[0].wait()
    node = table[pl.ds(0, nodes)]
    outgoing[...] = dot(send_hot, node).astype(BF16).reshape(4, slots, width)
    receiver_rows = dot(receiver_hot, node).astype(BF16)
    inputs_t[pl.ds(2 * width, width)] = jnp.transpose(receiver_rows)
    loads[1].wait()
    loads[2].wait()
    preact[...] = (
        dot(edge[...], w_first[pl.ds(0, width)])
        + dot(receiver_rows, w_first[pl.ds(2 * width, width)])
        + vectors[0:1]
    )
    pl.semaphore_wait(barrier, len(peers))
    halo = [
        comm.copy(outgoing.at[k], table.at[pl.ds(nodes + k * slots, slots)], to)
        for k, to in enumerate(
            (wide_neighbour(1), wide_neighbour(-1), narrow_neighbour(1), narrow_neighbour(-1))
        )
    ]
    inputs_t[pl.ds(0, width)] = jnp.transpose(edge[...])
    from_sender[...] = hot_columns(sender_row, table.shape[0])
    loads[3].wait()
    upstream[...] = dot(receiver_hot, cot[...])
    loads[4].wait()
    weight_sq[...] = slab_rows(jnp.square(w_first[...].astype(F32)), jnp.square(w_second[...].astype(F32)))
    for copy in halo:
        copy.wait_recv()
    for i in range(edges // ROWS):
        rows = pl.ds(i * ROWS, ROWS)
        sender_rows = dot(from_sender[rows], table[...]).astype(BF16)
        inputs_t[pl.ds(width, width), rows] = jnp.transpose(sender_rows)
        pre = preact[rows] + dot(sender_rows, w_first[pl.ds(width, width)])
        sigma = 1.0 / (1.0 + jnp.exp(-pre))
        activation = (pre * sigma).astype(BF16)
        activation_t[:, rows] = jnp.transpose(activation)
        slope = sigma * (1.0 + pre * (1.0 - sigma))
        second_pre = dot(activation, w_second[...]) + vectors[1:2]
        centered = second_pre - jnp.mean(second_pre, -1, keepdims=True)
        variance = jnp.mean(centered * centered, -1, keepdims=True)
        inv_std = lax.rsqrt(variance + 1e-05)
        normalized = centered * inv_std
        scaled = upstream[rows] * vectors[2:3]
        back = (
            inv_std
            * (
                scaled
                - jnp.mean(scaled, -1, keepdims=True)
                - normalized * jnp.mean(scaled * normalized, -1, keepdims=True)
            )
        ).astype(BF16)
        norm_back[rows] = back
        pre_back[rows] = (dot_nt(back, w_second[...]) * slope).astype(BF16)

    other = 1 - c
    first_rows, second_rows = pl.ds(0, first_out.shape[0]), pl.ds(first_out.shape[0], second_out.shape[0])
    for half, out_a, out_b in ((other, sent_a, sent_b), (c, own_a, own_b)):
        columns = pl.ds(pl.multiple_of(half * 256, 256), 256)
        split_blocks(dot(activation_t[...], norm_back[:, columns]), out_a, out_b, second_rows)
        split_blocks(dot(inputs_t[...], pre_back[:, columns]), out_a, out_b, first_rows)
        if out_a is sent_a:
            pair = [
                comm.copy(sent_a, from_core_a, {"c": other}),
                comm.copy(sent_b, from_core_b, {"c": other}),
            ]
    for copy in pair:
        copy.wait_recv()
    rings = (
        Ring(comm, "y", own_a, from_core_a, staged_a, ring_a),
        Ring(comm, "z", own_b, from_core_b, staged_b, ring_b),
    )

    def table_part():
        sums = dot(hot_rows(sender_row, table.shape[0]), pre_back[...]).astype(BF16)
        grads = dot_nt(sums, w_first[pl.ds(width, width)])
        local_grad[...] = grads[:nodes]
        halo_grad[...] = grads[nodes:].astype(BF16).reshape(4, slots, width)

    def receiver_part():
        sums = dot(hot_rows(receiver_row, nodes), pre_back[...]).astype(BF16)
        local_grad[...] += dot_nt(sums, w_first[pl.ds(2 * width, width)]) + cot[...].astype(F32)

    def edge_part():
        edge_grad_out[...] = (upstream[...] + dot_nt(pre_back[...], w_first[pl.ds(0, width)])).astype(BF16)

    work = [table_part, receiver_part, edge_part]
    for step in range(max(nz, ny) // 2):
        for ring in rings:
            ring.step(step)
        if work:
            work.pop(0)()
    for rest in work:
        rest()
    rings[0].finish(over_a, over_sent_a)
    to_z = scatter(comm, "z", lambda peer: over_sent_a.at[peer], cross_a)
    rings[1].finish(over_b, over_sent_b)
    to_y = scatter(comm, "y", lambda peer: over_sent_b.at[peer], cross_b)
    share[0] = total_of(to_z, over_a[lax.axis_index("z")], cross_a).astype(BF16)
    share[1] = total_of(to_y, over_b[lax.axis_index("y")], cross_b).astype(BF16)
    here = lax.axis_index("x") * 2 + c
    shares[here] = share[...]
    copies = [comm.copy(share, shares.at[here], device) for device in narrow_peers()]
    for copy in copies:
        copy.wait_recv()
    slabs = []
    for core in (0, 1):
        for i in (0, 1):
            value = shares[core, i].astype(F32)
            for x in range(1, across):
                value = value + shares[2 * x + core, i].astype(F32)
            slabs.append(value)
    cut = first_out.shape[0]
    grads = jnp.concatenate(slabs, 1)
    square = grads * grads
    squares[0] = slab_rows(square[:cut], square[cut:])
    copies = scatter(comm, "y", lambda peer: squares.at[0], squares_in.at[pl.ds(0, ny - 1)])
    halo = [
        comm.copy(halo_grad.at[k], returned.at[k], to)
        for k, to in enumerate(
            (wide_neighbour(-1), wide_neighbour(1), narrow_neighbour(-1), narrow_neighbour(1))
        )
    ]
    squares[1] = total_of(copies, squares[0], squares_in.at[pl.ds(0, ny - 1)])
    copies = scatter(comm, "z", lambda peer: squares.at[1], squares_in.at[pl.ds(ny - 1, nz - 1)])
    for copy in halo:
        copy.wait_recv()
    node_grad_out[...] = (
        local_grad[...] + dot(hot_rows(send_row, nodes), returned[...].reshape(4 * slots, width))
    ).astype(BF16)
    grad_sq = total_of(copies, squares[1], squares_in.at[pl.ds(ny - 1, nz - 1)])
    factors = [clip_rows(grad_sq, weight_sq[...], which) for which in (0, 1)]
    for i in range(4):
        columns = slice(128 * i, 128 * (i + 1))
        first = factors[0][2 * i : 2 * i + 1] * math.sqrt(cut * nz * ny)
        second = factors[1][2 * i + 1 : 2 * i + 2] * math.sqrt(second_out.shape[0] * nz * ny)
        first_out[:, columns] = grads[:cut, columns] * first
        second_out[:, columns] = grads[cut:, columns] * second
    comm.drain()


def per_device(
    node_latent,
    edge_latent,
    node_cotangent,
    w_first,
    bias_first,
    w_second,
    bias_second,
    norm_gain,
    send_map,
    edge_sender,
    edge_receiver,
):
    nz, ny, across = lax.axis_size("z"), lax.axis_size("y"), lax.axis_size("x")
    nodes, width = node_latent.shape
    edges = edge_latent.shape[0]
    slots = send_map.shape[2]
    table_rows = nodes + 4 * slots
    first_rows, second_rows = w_first.shape[0] // (nz * ny), w_second.shape[0] // (nz * ny)
    rows = first_rows + second_rows
    ids = jnp.concatenate([send_map.reshape(4 * slots), edge_sender, edge_receiver]).reshape(1, -1)
    vectors = jnp.stack([bias_first, bias_second, norm_gain]).astype(F32)
    vmem = pl.BlockSpec(memory_space=pltpu.VMEM)
    hbm = pl.BlockSpec(memory_space=pl.ANY)
    ring_copies = 2 * (ny - 1) + 2 * (nz - 1)
    copies = 8 + 2 + ring_copies + (nz - 1 + ny - 1) + 2 * across - 1 + ny - 1 + nz - 1
    return pl.pallas_call(
        kernel,
        out_shape=(
            jax.ShapeDtypeStruct((nodes, width), BF16),
            jax.ShapeDtypeStruct((edges, width), BF16),
            jax.ShapeDtypeStruct((first_rows, width), F32),
            jax.ShapeDtypeStruct((second_rows, width), F32),
        ),
        in_specs=[vmem] * 2 + [hbm] * 5,
        out_specs=(vmem,) * 4,
        scratch_shapes=[
            pltpu.VMEM((table_rows, width), BF16),
            pltpu.VMEM((edges, width), BF16),
            pltpu.VMEM((nodes, width), BF16),
            pltpu.VMEM((3 * width, width), BF16),
            pltpu.VMEM((width, width), BF16),
            pltpu.VMEM((4, slots, width), BF16),
            pltpu.VMEM((3 * width, edges), BF16),
            pltpu.VMEM((edges, width), F32),
            pltpu.VMEM((edges, width), F32),
            pltpu.VMEM((width, edges), BF16),
            pltpu.VMEM((edges, width), BF16),
            pltpu.VMEM((edges, width), BF16),
            pltpu.VMEM((edges, table_rows), BF16),
            pltpu.VMEM((8, 128), F32),
            pltpu.VMEM((4, slots, width), BF16),
            pltpu.VMEM((4, slots, width), BF16),
            pltpu.VMEM((nodes, width), F32),
            pltpu.VMEM((ny, nz, rows, 128), BF16),
            pltpu.VMEM((nz, ny, rows, 128), BF16),
            pltpu.VMEM((ny, nz, rows, 128), BF16),
            pltpu.VMEM((nz, ny, rows, 128), BF16),
            pltpu.VMEM((ny, nz, rows, 128), F32),
            pltpu.VMEM((nz, ny, rows, 128), F32),
            pltpu.VMEM((2 * (ny - 1), nz // 2, rows, 128), BF16),
            pltpu.VMEM((2 * (nz - 1), ny // 2, rows, 128), BF16),
            pltpu.VMEM((2 * (ny - 1), nz // 2, rows, 128), BF16),
            pltpu.VMEM((2 * (nz - 1), ny // 2, rows, 128), BF16),
            pltpu.VMEM((nz, rows, 128), F32),
            pltpu.VMEM((ny, rows, 128), F32),
            pltpu.VMEM((nz, rows, 128), BF16),
            pltpu.VMEM((ny, rows, 128), BF16),
            pltpu.VMEM((nz - 1, rows, 128), BF16),
            pltpu.VMEM((ny - 1, rows, 128), BF16),
            pltpu.VMEM((2, rows, 128), BF16),
            pltpu.VMEM((2 * across, 2, rows, 128), BF16),
            pltpu.VMEM((2, 8, 128), F32),
            pltpu.VMEM((ny - 1 + nz - 1, 8, 128), F32),
            pltpu.SemaphoreType.DMA((5,)),
            pltpu.SemaphoreType.DMA((copies,)),
            pltpu.SemaphoreType.DMA((copies,)),
        ],
        compiler_params=pltpu.CompilerParams(
            collective_id=0, has_side_effects=True, vmem_limit_bytes=56 << 20
        ),
    )(ids, vectors, node_latent, edge_latent, node_cotangent, w_first, w_second)


def solution(mesh):
    finer = Mesh(mesh.devices.reshape(8, 8, 4, 2), ALL)
    in_specs = (
        P(ALL, None),
        P(ALL, None),
        P(ALL, None),
        P(),
        P(),
        P(),
        P(),
        P(),
        P(ALL, None, None),
        P(ALL),
        P(ALL),
    )
    out_specs = (P(ALL, None), P(ALL, None), P(WIDE, None), P(WIDE, None))
    return jax.shard_map(
        per_device, mesh=finer, in_specs=in_specs, out_specs=out_specs, check_vma=False
    )
```

```python
import math

import jax
import jax.numpy as jnp
from jax import lax
from jax.experimental import pallas as pl
from jax.experimental.pallas import tpu as pltpu
from jax.sharding import Mesh
from jax.sharding import PartitionSpec as P

WIDE = ("z", "y")
ALL = ("z", "y", "x", "c")
MESH = pl.DeviceIdType.MESH
F32 = jnp.float32
BF16 = jnp.bfloat16
ROWS = 256


def dot(a, b):
    return jnp.dot(a, b, preferred_element_type=F32)


def dot_nt(a, b):
    return lax.dot_general(a, b, (((1,), (1,)), ((), ())), preferred_element_type=F32)


class Comm:
    def __init__(self, send_sems, recv_sems):
        self.send_sems, self.recv_sems, self.groups, self.used = send_sems, recv_sems, [], 0

    def group(self, sent):
        self.groups.append(sent)
        return len(self.groups) - 1

    def recv_sem(self):
        self.used += 1
        return self.recv_sems.at[self.used - 1]

    def copy(self, group, src, dst, to, recv_sem=None):
        copy = pltpu.make_async_remote_copy(
            src_ref=src,
            dst_ref=dst,
            send_sem=self.send_sems.at[group],
            recv_sem=self.recv_sem() if recv_sem is None else recv_sem,
            device_id=to,
            device_id_type=MESH,
        )
        copy.start()
        return copy

    def drain(self):
        for i, sent in enumerate(self.groups):
            wait_for(sent, self.send_sems.at[i])


def wait_for(ref, sem):
    pltpu.make_async_copy(ref, ref, sem).wait()


class Ring:
    def __init__(self, comm, axis, sent, paired, own, staged, slots):
        self.comm, self.axis, self.sent, self.paired, self.own = comm, axis, sent, paired, own
        self.count, self.me = lax.axis_size(axis), lax.axis_index(axis)
        self.half = own.shape[1] // 2
        self.chains = []
        used = 0
        for half in (0, 1):
            for sign in (-1, 1):
                hops = self.count // 2 - (0 if (sign < 0) == (half == 0) else 1)
                span = pl.ds(used, max(hops, 1))
                self.chains.append((half, sign, hops, staged.at[span], slots.at[span]))
                used += hops
        self.last = [None] * 4
        self.staged = staged
        self.pairs = {}
        self.pair_group = comm.group(sent)

    def at(self, offset):
        return lax.rem(self.me + offset + self.count, self.count)

    def pair(self, offset, other):
        owner = self.at(offset)
        self.pairs[offset % self.count] = self.comm.copy(
            self.pair_group, self.sent.at[owner], self.paired.at[owner], {"c": other}
        )

    def value(self, offset, half):
        pair = self.pairs.pop(offset % self.count, None)
        if pair is not None:
            pair.wait_recv()
        owner = self.at(offset)
        part = pl.ds(half * self.half, self.half)
        return self.own[owner, part] + self.paired[owner, part].astype(F32)

    def step(self, step):
        if step == 0:
            self.group = self.comm.group(self.staged)
        for i, (half, sign, hops, staged, slots) in enumerate(self.chains):
            if step >= hops:
                continue
            value = self.value(sign * (hops - step), half)
            if step:
                self.last[i].wait_recv()
                value = value + slots[step - 1].astype(F32)
            staged[step] = value.astype(BF16)
            self.last[i] = self.comm.copy(
                self.group, staged.at[step], slots.at[step], {self.axis: self.at(sign)}
            )

    def finish(self, over, over_sent):
        for half in (0, 1):
            value = self.value(0, half)
            for i, (chain_half, _, hops, _, slots) in enumerate(self.chains):
                if chain_half == half and hops:
                    self.last[i].wait_recv()
                    value = value + slots[hops - 1].astype(F32)
            part = pl.ds(half * self.half, self.half)
            over[part] = value
            over_sent[part] = value.astype(BF16)


def offsets(count):
    return sorted(range(1, count), key=lambda k: -min(k, count - k))


def scatter(comm, axis, parts, slots):
    count, me = lax.axis_size(axis), lax.axis_index(axis)
    sem, group = comm.recv_sem(), comm.group(slots)
    for k in offsets(count):
        peer = lax.rem(me + k, count)
        comm.copy(group, parts(peer), slots.at[k - 1], {axis: peer}, sem)
    return slots, sem


def total_of(arriving, own):
    slots, sem = arriving
    wait_for(slots, sem)
    value = own
    for k in range(slots.shape[0]):
        value = value + slots[k].astype(F32)
    return value


def narrow_peers():
    across, cores = lax.axis_size("x"), lax.axis_size("c")
    x, c = lax.axis_index("x"), lax.axis_index("c")
    steps = offsets(across) + [0]
    return [
        {"x": lax.rem(x + i, across), "c": lax.rem(c + j, cores)}
        for i in steps
        for j in range(cores)
        if i or j
    ]


def wide_neighbour(step):
    nz, ny = lax.axis_size("z"), lax.axis_size("y")
    index = lax.rem(lax.axis_index("z") * ny + lax.axis_index("y") + step + nz * ny, nz * ny)
    return {"z": index // ny, "y": lax.rem(index, ny)}


def narrow_neighbour(step):
    across, cores = lax.axis_size("x"), lax.axis_size("c")
    count = across * cores
    index = lax.rem(lax.axis_index("x") * cores + lax.axis_index("c") + step + count, count)
    return {"x": index // cores, "c": lax.rem(index, cores)}


def greeted():
    found = [wide_neighbour(1), wide_neighbour(-1)]
    for axis in ("z", "y"):
        count, me = lax.axis_size(axis), lax.axis_index(axis)
        found += [{axis: lax.rem(me + k, count)} for k in offsets(count)]
    return found + narrow_peers()


def as_columns(row):
    blocks = [
        jnp.transpose(jnp.broadcast_to(row[:, 128 * i : 128 * (i + 1)], (128, 128)))
        for i in range(row.shape[1] // 128)
    ]
    return jnp.concatenate(blocks, 0)


def hot_rows(row, count):
    ids = lax.broadcasted_iota(jnp.int32, (count, row.shape[1]), 0)
    return jnp.where(ids == row, 1.0, 0.0).astype(BF16)


def hot_columns(row, count):
    columns = as_columns(row)
    ids = lax.broadcasted_iota(jnp.int32, columns.shape, 1)
    blocks = [jnp.where(columns == ids + 128 * i, 1.0, 0.0) for i in range(count // 128)]
    return jnp.concatenate(blocks, 1).astype(BF16)


def clip_rows(grad_sq, weight_sq, which):
    ratio = jnp.sqrt((grad_sq + 1e-06) / (weight_sq + 1e-06))
    rows = lax.broadcasted_iota(jnp.int32, ratio.shape, 0)
    mine = lax.rem(rows, 2) == which
    mean_ratio = jnp.sum(jnp.where(mine, ratio, 0.0)) / (ratio.shape[0] // 2 * ratio.shape[1])
    return jnp.minimum(1.0 / (mean_ratio * jnp.sqrt(weight_sq + 1e-06)), 1.0 / jnp.sqrt(grad_sq + 1e-06))


def slab_rows(first, second):
    rows = []
    for i in range(4):
        columns = slice(128 * i, 128 * (i + 1))
        rows += [
            jnp.sum(first[:, columns], 0, keepdims=True),
            jnp.sum(second[:, columns], 0, keepdims=True),
        ]
    return jnp.concatenate(rows, 0)


def split_blocks(value, out_a, out_b, rows):
    ny, nz = out_a.shape[:2]
    height = value.shape[0] // (ny * nz)
    lower = value[:, :128].reshape(nz, ny, height, 128)
    for y in range(ny):
        out_a[y, :, rows, :] = lower[:, y].astype(out_a.dtype)
    out_b[:, :, rows, :] = value[:, 128:].reshape(nz, ny, height, 128).astype(out_b.dtype)


def kernel(
    send_hbm,
    sender_hbm,
    receiver_hbm,
    bias_first_hbm,
    bias_second_hbm,
    gain_hbm,
    node_hbm,
    edge_hbm,
    cot_hbm,
    w_first_hbm,
    w_second_hbm,
    node_grad_hbm,
    edge_grad_hbm,
    first_hbm,
    second_hbm,
    send_map,
    sender_ids,
    receiver_ids,
    bias_first,
    bias_second,
    norm_gain,
    table,
    edge,
    cot,
    w_first,
    w_second,
    outgoing,
    inputs_t,
    preact,
    upstream,
    activation_t,
    norm_back,
    pre_back,
    from_sender,
    weight_sq,
    halo_grad,
    returned,
    local_grad,
    sent_a,
    sent_b,
    from_core_a,
    from_core_b,
    own_a,
    own_b,
    staged_a,
    staged_b,
    ring_a,
    ring_b,
    over_a,
    over_b,
    over_sent_a,
    over_sent_b,
    cross_a,
    cross_b,
    share,
    shares,
    squares,
    squares_in,
    node_grad_out,
    edge_grad_out,
    first_out,
    second_out,
    load_sems,
    store_sems,
    send_sems,
    recv_sems,
):
    comm = Comm(send_sems, recv_sems)
    c = lax.axis_index("c")
    nz, ny, across = lax.axis_size("z"), lax.axis_size("y"), lax.axis_size("x")
    nodes, width = node_hbm.shape
    edges = edge_hbm.shape[0]
    slots = outgoing.shape[1]
    barrier = pltpu.get_barrier_semaphore()
    peers = greeted()
    for peer in peers:
        pl.semaphore_signal(barrier, 1, device_id=peer, device_id_type=MESH)
    loads = [
        pltpu.make_async_copy(src, dst, load_sems.at[i])
        for i, (src, dst) in enumerate(
            (
                (send_hbm, send_map),
                (node_hbm, table.at[pl.ds(0, nodes)]),
                (receiver_hbm, receiver_ids),
                (edge_hbm, edge),
                (w_first_hbm, w_first),
                (bias_first_hbm, bias_first),
                (sender_hbm, sender_ids),
                (cot_hbm, cot),
                (w_second_hbm, w_second),
                (bias_second_hbm, bias_second),
                (gain_hbm, norm_gain),
            )
        )
    ]
    for load in loads:
        load.start()
    loads[0].wait()
    send_row = jnp.concatenate([send_map[0, k : k + 1, :] for k in range(4)], 1)
    send_hot = hot_columns(send_row, nodes)
    loads[1].wait()
    node = table[pl.ds(0, nodes)]
    outgoing[...] = dot(send_hot, node).astype(BF16).reshape(4, slots, width)
    pl.semaphore_wait(barrier, len(peers))
    halo_sem, halo_group = comm.recv_sem(), comm.group(outgoing)
    arriving = table.at[pl.ds(nodes, 4 * slots)]
    for k, to in enumerate(
        (wide_neighbour(1), wide_neighbour(-1), narrow_neighbour(1), narrow_neighbour(-1))
    ):
        comm.copy(halo_group, outgoing.at[k], table.at[pl.ds(nodes + k * slots, slots)], to, halo_sem)
    loads[2].wait()
    receiver_row = receiver_ids[...].reshape(1, edges)
    receiver_hot = hot_columns(receiver_row, nodes)
    receiver_rows = dot(receiver_hot, node).astype(BF16)
    inputs_t[pl.ds(2 * width, width)] = jnp.transpose(receiver_rows)
    for load in loads[3:]:
        load.wait()
    vectors = [v[...].astype(F32).reshape(1, width) for v in (bias_first, bias_second, norm_gain)]
    preact[...] = (
        dot(edge[...], w_first[pl.ds(0, width)])
        + dot(receiver_rows, w_first[pl.ds(2 * width, width)])
        + vectors[0]
    )
    sender_row = sender_ids[...].reshape(1, edges)
    inputs_t[pl.ds(0, width)] = jnp.transpose(edge[...])
    from_sender[...] = hot_columns(sender_row, table.shape[0])
    upstream[...] = dot(receiver_hot, cot[...])
    weight_sq[...] = slab_rows(jnp.square(w_first[...].astype(F32)), jnp.square(w_second[...].astype(F32)))
    wait_for(arriving, halo_sem)
    for i in range(edges // ROWS):
        rows = pl.ds(i * ROWS, ROWS)
        sender_rows = dot(from_sender[rows], table[...]).astype(BF16)
        inputs_t[pl.ds(width, width), rows] = jnp.transpose(sender_rows)
        pre = preact[rows] + dot(sender_rows, w_first[pl.ds(width, width)])
        sigma = 1.0 / (1.0 + jnp.exp(-pre))
        activation = (pre * sigma).astype(BF16)
        activation_t[:, rows] = jnp.transpose(activation)
        slope = sigma * (1.0 + pre * (1.0 - sigma))
        second_pre = dot(activation, w_second[...]) + vectors[1]
        centered = second_pre - jnp.mean(second_pre, -1, keepdims=True)
        variance = jnp.mean(centered * centered, -1, keepdims=True)
        inv_std = lax.rsqrt(variance + 1e-05)
        normalized = centered * inv_std
        scaled = upstream[rows] * vectors[2]
        back = (
            inv_std
            * (
                scaled
                - jnp.mean(scaled, -1, keepdims=True)
                - normalized * jnp.mean(scaled * normalized, -1, keepdims=True)
            )
        ).astype(BF16)
        norm_back[rows] = back
        pre_back[rows] = (dot_nt(back, w_second[...]) * slope).astype(BF16)

    other = 1 - c
    rings = (
        Ring(comm, "y", sent_a, from_core_a, own_a, staged_a, ring_a),
        Ring(comm, "z", sent_b, from_core_b, own_b, staged_b, ring_b),
    )
    cut, rest = first_out.shape[0], second_out.shape[0]
    for half, out_a, out_b in ((other, sent_a, sent_b), (c, own_a, own_b)):
        columns = pl.ds(pl.multiple_of(half * 256, 256), 256)
        split_blocks(dot(activation_t[...], norm_back[:, columns]), out_a, out_b, pl.ds(cut, rest))
        split_blocks(dot(inputs_t[...], pre_back[:, columns]), out_a, out_b, pl.ds(0, cut))
        if out_a is sent_a:
            for i in range(max(ny, nz)):
                for ring in rings:
                    order = offsets(ring.count) + [0]
                    if i < ring.count:
                        ring.pair(order[i], other)

    def table_part():
        sums = dot(hot_rows(sender_row, table.shape[0]), pre_back[...]).astype(BF16)
        grads = dot_nt(sums, w_first[pl.ds(width, width)])
        local_grad[...] = grads[:nodes]
        halo_grad[...] = grads[nodes:].astype(BF16).reshape(4, slots, width)

    def receiver_part():
        sums = dot(hot_rows(receiver_row, nodes), pre_back[...]).astype(BF16)
        local_grad[...] += dot_nt(sums, w_first[pl.ds(2 * width, width)]) + cot[...].astype(F32)

    stores = []

    def store(src, dst):
        copy = pltpu.make_async_copy(src, dst, store_sems.at[len(stores)])
        copy.start()
        stores.append(copy)

    def edge_part():
        edge_grad_out[...] = (upstream[...] + dot_nt(pre_back[...], w_first[pl.ds(0, width)])).astype(BF16)
        store(edge_grad_out, edge_grad_hbm)

    work = [table_part, receiver_part, edge_part]
    for step in range(max(nz, ny) // 2):
        for ring in rings:
            ring.step(step)
        if work:
            work.pop(0)()
    for part in work:
        part()
    rings[0].finish(over_a, over_sent_a)
    to_z = scatter(comm, "z", lambda peer: over_sent_a.at[peer], cross_a)
    rings[1].finish(over_b, over_sent_b)
    to_y = scatter(comm, "y", lambda peer: over_sent_b.at[peer], cross_b)
    share[0] = total_of(to_z, over_a[lax.axis_index("z")]).astype(BF16)
    share[1] = total_of(to_y, over_b[lax.axis_index("y")]).astype(BF16)
    here = lax.axis_index("x") * 2 + c
    shares[here] = share[...]
    group = comm.group(shares.at[pl.ds(0, 2 * across - 1)])
    copies = [comm.copy(group, share, shares.at[here], device) for device in narrow_peers()]
    for copy in copies:
        copy.wait_recv()
    slabs = []
    for core in (0, 1):
        for i in (0, 1):
            value = shares[core, i].astype(F32)
            for x in range(1, across):
                value = value + shares[2 * x + core, i].astype(F32)
            slabs.append(value)
    grads = jnp.concatenate(slabs, 1)
    square = grads * grads
    squares[0] = slab_rows(square[:cut], square[cut:])
    to_y = scatter(comm, "y", lambda peer: squares.at[0], squares_in.at[pl.ds(0, ny - 1)])
    back_sem, back_group = comm.recv_sem(), comm.group(halo_grad)
    for k, to in enumerate(
        (wide_neighbour(-1), wide_neighbour(1), narrow_neighbour(-1), narrow_neighbour(1))
    ):
        comm.copy(back_group, halo_grad.at[k], returned.at[k], to, back_sem)
    squares[1] = total_of(to_y, squares[0])
    to_z = scatter(comm, "z", lambda peer: squares.at[1], squares_in.at[pl.ds(ny - 1, nz - 1)])
    wait_for(returned, back_sem)
    node_grad_out[...] = (
        local_grad[...] + dot(hot_rows(send_row, nodes), returned[...].reshape(4 * slots, width))
    ).astype(BF16)
    store(node_grad_out, node_grad_hbm)
    grad_sq = total_of(to_z, squares[1])
    factors = [clip_rows(grad_sq, weight_sq[...], which) for which in (0, 1)]
    for i in range(4):
        columns = slice(128 * i, 128 * (i + 1))
        first = factors[0][2 * i : 2 * i + 1] * math.sqrt(cut * nz * ny)
        second = factors[1][2 * i + 1 : 2 * i + 2] * math.sqrt(rest * nz * ny)
        first_out[:, columns] = grads[:cut, columns] * first
        second_out[:, columns] = grads[cut:, columns] * second
    store(first_out, first_hbm)
    store(second_out, second_hbm)
    comm.drain()
    for copy in stores:
        copy.wait()


def deliver(*refs):
    count = len(refs) // 2
    copies = [
        pltpu.make_async_copy(refs[i], refs[count + i], refs[-1].at[i]) for i in range(count)
    ]
    for copy in copies:
        copy.start()
    for copy in copies:
        copy.wait()


def per_device(
    node_latent,
    edge_latent,
    node_cotangent,
    w_first,
    bias_first,
    w_second,
    bias_second,
    norm_gain,
    send_map,
    edge_sender,
    edge_receiver,
):
    nz, ny, across = lax.axis_size("z"), lax.axis_size("y"), lax.axis_size("x")
    nodes, width = node_latent.shape
    edges = edge_latent.shape[0]
    slots = send_map.shape[2]
    table_rows = nodes + 4 * slots
    first_rows, second_rows = w_first.shape[0] // (nz * ny), w_second.shape[0] // (nz * ny)
    rows = first_rows + second_rows
    vmem = pl.BlockSpec(memory_space=pltpu.VMEM)
    hbm = pl.BlockSpec(memory_space=pltpu.HBM)
    copies = 1 + 3 * (ny + nz) - 4 + 2 + 2 * across - 1 + 3
    results = pl.pallas_call(
        kernel,
        out_shape=(
            jax.ShapeDtypeStruct((nodes, width), BF16),
            jax.ShapeDtypeStruct((edges, width), BF16),
            jax.ShapeDtypeStruct((first_rows, width), F32),
            jax.ShapeDtypeStruct((second_rows, width), F32),
        ),
        in_specs=[hbm] * 11,
        out_specs=(hbm,) * 4,
        scratch_shapes=[
            pltpu.VMEM(send_map.shape, jnp.int32),
            pltpu.VMEM((edges,), jnp.int32),
            pltpu.VMEM((edges,), jnp.int32),
            pltpu.VMEM((width,), BF16),
            pltpu.VMEM((width,), BF16),
            pltpu.VMEM((width,), BF16),
            pltpu.VMEM((table_rows, width), BF16),
            pltpu.VMEM((edges, width), BF16),
            pltpu.VMEM((nodes, width), BF16),
            pltpu.VMEM((3 * width, width), BF16),
            pltpu.VMEM((width, width), BF16),
            pltpu.VMEM((4, slots, width), BF16),
            pltpu.VMEM((3 * width, edges), BF16),
            pltpu.VMEM((edges, width), F32),
            pltpu.VMEM((edges, width), F32),
            pltpu.VMEM((width, edges), BF16),
            pltpu.VMEM((edges, width), BF16),
            pltpu.VMEM((edges, width), BF16),
            pltpu.VMEM((edges, table_rows), BF16),
            pltpu.VMEM((8, 128), F32),
            pltpu.VMEM((4, slots, width), BF16),
            pltpu.VMEM((4, slots, width), BF16),
            pltpu.VMEM((nodes, width), F32),
            pltpu.VMEM((ny, nz, rows, 128), BF16),
            pltpu.VMEM((nz, ny, rows, 128), BF16),
            pltpu.VMEM((ny, nz, rows, 128), BF16),
            pltpu.VMEM((nz, ny, rows, 128), BF16),
            pltpu.VMEM((ny, nz, rows, 128), F32),
            pltpu.VMEM((nz, ny, rows, 128), F32),
            pltpu.VMEM((2 * (ny - 1), nz // 2, rows, 128), BF16),
            pltpu.VMEM((2 * (nz - 1), ny // 2, rows, 128), BF16),
            pltpu.VMEM((2 * (ny - 1), nz // 2, rows, 128), BF16),
            pltpu.VMEM((2 * (nz - 1), ny // 2, rows, 128), BF16),
            pltpu.VMEM((nz, rows, 128), F32),
            pltpu.VMEM((ny, rows, 128), F32),
            pltpu.VMEM((nz, rows, 128), BF16),
            pltpu.VMEM((ny, rows, 128), BF16),
            pltpu.VMEM((nz - 1, rows, 128), BF16),
            pltpu.VMEM((ny - 1, rows, 128), BF16),
            pltpu.VMEM((2, rows, 128), BF16),
            pltpu.VMEM((2 * across, 2, rows, 128), BF16),
            pltpu.VMEM((2, 8, 128), F32),
            pltpu.VMEM((ny - 1 + nz - 1, 8, 128), F32),
            pltpu.VMEM((nodes, width), BF16),
            pltpu.VMEM((edges, width), BF16),
            pltpu.VMEM((first_rows, width), F32),
            pltpu.VMEM((second_rows, width), F32),
            pltpu.SemaphoreType.DMA((11,)),
            pltpu.SemaphoreType.DMA((4,)),
            pltpu.SemaphoreType.DMA((11,)),
            pltpu.SemaphoreType.DMA((copies,)),
        ],
        compiler_params=pltpu.CompilerParams(
            collective_id=0, has_side_effects=True, vmem_limit_bytes=56 << 20
        ),
    )(
        send_map,
        edge_sender,
        edge_receiver,
        bias_first,
        bias_second,
        norm_gain,
        node_latent,
        edge_latent,
        node_cotangent,
        w_first,
        w_second,
    )
    return pl.pallas_call(
        deliver,
        out_shape=[jax.ShapeDtypeStruct(v.shape, v.dtype) for v in results],
        in_specs=[vmem] * 4,
        out_specs=[hbm] * 4,
        scratch_shapes=[pltpu.SemaphoreType.DMA((4,))],
        compiler_params=pltpu.CompilerParams(vmem_limit_bytes=8 << 20),
    )(*results)


def solution(mesh):
    finer = Mesh(mesh.devices.reshape(8, 8, 4, 2), ALL)
    in_specs = (
        P(ALL, None),
        P(ALL, None),
        P(ALL, None),
        P(),
        P(),
        P(),
        P(),
        P(),
        P(ALL, None, None),
        P(ALL),
        P(ALL),
    )
    out_specs = (P(ALL, None), P(ALL, None), P(WIDE, None), P(WIDE, None))
    return jax.shard_map(
        per_device, mesh=finer, in_specs=in_specs, out_specs=out_specs, check_vma=False
    )
```

```python
import math

import jax
import jax.numpy as jnp
from jax import lax
from jax.experimental import pallas as pl
from jax.experimental.pallas import tpu as pltpu
from jax.sharding import Mesh
from jax.sharding import PartitionSpec as P

WIDE = ("z", "y")
ALL = ("z", "y", "x", "c")
MESH = pl.DeviceIdType.MESH
F32 = jnp.float32
BF16 = jnp.bfloat16
ROWS = 256


def dot(a, b):
    return jnp.dot(a, b, preferred_element_type=F32)


def dot_nt(a, b):
    return lax.dot_general(a, b, (((1,), (1,)), ((), ())), preferred_element_type=F32)


class Comm:
    def __init__(self, send_sems, recv_sems):
        self.send_sems, self.recv_sems, self.groups, self.used = send_sems, recv_sems, [], 0

    def group(self, sent):
        self.groups.append(sent)
        return len(self.groups) - 1

    def recv_sem(self):
        self.used += 1
        return self.recv_sems.at[self.used - 1]

    def copy(self, group, src, dst, to, recv_sem=None):
        copy = pltpu.make_async_remote_copy(
            src_ref=src,
            dst_ref=dst,
            send_sem=self.send_sems.at[group],
            recv_sem=self.recv_sem() if recv_sem is None else recv_sem,
            device_id=to,
            device_id_type=MESH,
        )
        copy.start()
        return copy

    def drain(self):
        for i, sent in enumerate(self.groups):
            wait_for(sent, self.send_sems.at[i])


def wait_for(ref, sem):
    pltpu.make_async_copy(ref, ref, sem).wait()


class Ring:
    def __init__(self, comm, axis, sent, paired, own, staged, slots):
        self.comm, self.axis, self.sent, self.paired, self.own = comm, axis, sent, paired, own
        self.count, self.me = lax.axis_size(axis), lax.axis_index(axis)
        self.half = own.shape[1] // 2
        self.chains = []
        used = 0
        for half in (0, 1):
            for sign in (-1, 1):
                hops = self.count // 2 - (0 if (sign < 0) == (half == 0) else 1)
                span = pl.ds(used, max(hops, 1))
                self.chains.append((half, sign, hops, staged.at[span], slots.at[span]))
                used += hops
        self.last = [None] * 4
        self.staged = staged
        self.pairs = {}
        self.pair_group = comm.group(sent)

    def at(self, offset):
        return lax.rem(self.me + offset + self.count, self.count)

    def pair(self, offset, other):
        owner = self.at(offset)
        self.pairs[offset % self.count] = self.comm.copy(
            self.pair_group, self.sent.at[owner], self.paired.at[owner], {"c": other}
        )

    def value(self, offset, half):
        pair = self.pairs.pop(offset % self.count, None)
        if pair is not None:
            pair.wait_recv()
        owner = self.at(offset)
        part = pl.ds(half * self.half, self.half)
        return self.own[owner, part] + self.paired[owner, part].astype(F32)

    def step(self, step):
        if step == 0:
            self.group = self.comm.group(self.staged)
        for i, (half, sign, hops, staged, slots) in enumerate(self.chains):
            if step >= hops:
                continue
            value = self.value(sign * (hops - step), half)
            if step:
                self.last[i].wait_recv()
                value = value + slots[step - 1].astype(F32)
            staged[step] = value.astype(BF16)
            self.last[i] = self.comm.copy(
                self.group, staged.at[step], slots.at[step], {self.axis: self.at(sign)}
            )

    def finish(self, over, over_sent):
        for half in (0, 1):
            value = self.value(0, half)
            for i, (chain_half, _, hops, _, slots) in enumerate(self.chains):
                if chain_half == half and hops:
                    self.last[i].wait_recv()
                    value = value + slots[hops - 1].astype(F32)
            part = pl.ds(half * self.half, self.half)
            over[part] = value
            over_sent[part] = value.astype(BF16)


def offsets(count):
    return sorted(range(1, count), key=lambda k: -min(k, count - k))


def scatter(comm, axis, parts, slots):
    count, me = lax.axis_size(axis), lax.axis_index(axis)
    sem, group = comm.recv_sem(), comm.group(slots)
    for k in offsets(count):
        peer = lax.rem(me + k, count)
        comm.copy(group, parts(peer), slots.at[k - 1], {axis: peer}, sem)
    return slots, sem


def total_of(arriving, own):
    slots, sem = arriving
    wait_for(slots, sem)
    value = own
    for k in range(slots.shape[0]):
        value = value + slots[k].astype(F32)
    return value


def narrow_peers():
    across, cores = lax.axis_size("x"), lax.axis_size("c")
    x, c = lax.axis_index("x"), lax.axis_index("c")
    steps = offsets(across) + [0]
    return [
        {"x": lax.rem(x + i, across), "c": lax.rem(c + j, cores)}
        for i in steps
        for j in range(cores)
        if i or j
    ]


def wide_neighbour(step):
    nz, ny = lax.axis_size("z"), lax.axis_size("y")
    index = lax.rem(lax.axis_index("z") * ny + lax.axis_index("y") + step + nz * ny, nz * ny)
    return {"z": index // ny, "y": lax.rem(index, ny)}


def narrow_neighbour(step):
    across, cores = lax.axis_size("x"), lax.axis_size("c")
    count = across * cores
    index = lax.rem(lax.axis_index("x") * cores + lax.axis_index("c") + step + count, count)
    return {"x": index // cores, "c": lax.rem(index, cores)}


def greeted():
    found = [wide_neighbour(1), wide_neighbour(-1)]
    for axis in ("z", "y"):
        count, me = lax.axis_size(axis), lax.axis_index(axis)
        found += [{axis: lax.rem(me + k, count)} for k in sorted({1, count - 1})]
    return found + narrow_peers()


def as_columns(row):
    blocks = [
        jnp.transpose(jnp.broadcast_to(row[:, 128 * i : 128 * (i + 1)], (128, 128)))
        for i in range(row.shape[1] // 128)
    ]
    return jnp.concatenate(blocks, 0)


def hot_rows(row, count):
    ids = lax.broadcasted_iota(jnp.int32, (count, row.shape[1]), 0)
    return jnp.where(ids == row, 1.0, 0.0).astype(BF16)


def hot_columns(row, count):
    columns = as_columns(row)
    ids = lax.broadcasted_iota(jnp.int32, columns.shape, 1)
    blocks = [jnp.where(columns == ids + 128 * i, 1.0, 0.0) for i in range(count // 128)]
    return jnp.concatenate(blocks, 1).astype(BF16)


def clip_rows(grad_sq, weight_sq, which):
    ratio = jnp.sqrt((grad_sq + 1e-06) / (weight_sq + 1e-06))
    rows = lax.broadcasted_iota(jnp.int32, ratio.shape, 0)
    mine = lax.rem(rows, 2) == which
    mean_ratio = jnp.sum(jnp.where(mine, ratio, 0.0)) / (ratio.shape[0] // 2 * ratio.shape[1])
    return jnp.minimum(1.0 / (mean_ratio * jnp.sqrt(weight_sq + 1e-06)), 1.0 / jnp.sqrt(grad_sq + 1e-06))


def slab_rows(first, second):
    rows = []
    for i in range(4):
        columns = slice(128 * i, 128 * (i + 1))
        rows += [
            jnp.sum(first[:, columns], 0, keepdims=True),
            jnp.sum(second[:, columns], 0, keepdims=True),
        ]
    return jnp.concatenate(rows, 0)


def split_blocks(value, out_a, out_b, rows):
    ny, nz = out_a.shape[:2]
    height = value.shape[0] // (ny * nz)
    lower = value[:, :128].reshape(nz, ny, height, 128)
    for y in range(ny):
        out_a[y, :, rows, :] = lower[:, y].astype(out_a.dtype)
    out_b[:, :, rows, :] = value[:, 128:].reshape(nz, ny, height, 128).astype(out_b.dtype)


def kernel(
    send_hbm,
    sender_hbm,
    receiver_hbm,
    bias_first_hbm,
    bias_second_hbm,
    gain_hbm,
    node_hbm,
    edge_hbm,
    cot_hbm,
    w_first_hbm,
    w_second_hbm,
    node_grad_hbm,
    edge_grad_hbm,
    first_hbm,
    second_hbm,
    send_map,
    sender_ids,
    receiver_ids,
    bias_first,
    bias_second,
    norm_gain,
    table,
    edge,
    cot,
    w_first,
    w_second,
    outgoing,
    inputs_t,
    preact,
    upstream,
    activation_t,
    norm_back,
    pre_back,
    from_sender,
    weight_sq,
    halo_grad,
    returned,
    local_grad,
    sent_a,
    sent_b,
    from_core_a,
    from_core_b,
    own_a,
    own_b,
    staged_a,
    staged_b,
    ring_a,
    ring_b,
    over_a,
    over_b,
    over_sent_a,
    over_sent_b,
    cross_a,
    cross_b,
    share,
    shares,
    squares,
    squares_in,
    node_grad_out,
    edge_grad_out,
    first_out,
    second_out,
    load_sems,
    store_sems,
    send_sems,
    recv_sems,
):
    comm = Comm(send_sems, recv_sems)
    c = lax.axis_index("c")
    nz, ny, across = lax.axis_size("z"), lax.axis_size("y"), lax.axis_size("x")
    nodes, width = node_hbm.shape
    edges = edge_hbm.shape[0]
    slots = outgoing.shape[1]
    barrier = pltpu.get_barrier_semaphore()
    peers = greeted()
    for peer in peers:
        pl.semaphore_signal(barrier, 1, device_id=peer, device_id_type=MESH)
    loads = [
        pltpu.make_async_copy(src, dst, load_sems.at[i])
        for i, (src, dst) in enumerate(
            (
                (send_hbm, send_map),
                (node_hbm, table.at[pl.ds(0, nodes)]),
                (receiver_hbm, receiver_ids),
                (edge_hbm, edge),
                (w_first_hbm, w_first),
                (bias_first_hbm, bias_first),
                (sender_hbm, sender_ids),
                (cot_hbm, cot),
                (w_second_hbm, w_second),
                (bias_second_hbm, bias_second),
                (gain_hbm, norm_gain),
            )
        )
    ]
    for load in loads:
        load.start()
    loads[0].wait()
    send_row = jnp.concatenate([send_map[0, k : k + 1, :] for k in range(4)], 1)
    send_hot = hot_columns(send_row, nodes)
    loads[1].wait()
    node = table[pl.ds(0, nodes)]
    outgoing[...] = dot(send_hot, node).astype(BF16).reshape(4, slots, width)
    pl.semaphore_wait(barrier, len(peers))
    halo_sem, halo_group = comm.recv_sem(), comm.group(outgoing)
    arriving = table.at[pl.ds(nodes, 4 * slots)]
    for k, to in enumerate(
        (wide_neighbour(1), wide_neighbour(-1), narrow_neighbour(1), narrow_neighbour(-1))
    ):
        comm.copy(halo_group, outgoing.at[k], table.at[pl.ds(nodes + k * slots, slots)], to, halo_sem)
    loads[2].wait()
    receiver_row = receiver_ids[...].reshape(1, edges)
    receiver_hot = hot_columns(receiver_row, nodes)
    receiver_rows = dot(receiver_hot, node).astype(BF16)
    inputs_t[pl.ds(2 * width, width)] = jnp.transpose(receiver_rows)
    for load in loads[3:]:
        load.wait()
    vectors = [v[...].astype(F32).reshape(1, width) for v in (bias_first, bias_second, norm_gain)]
    preact[...] = (
        dot(edge[...], w_first[pl.ds(0, width)])
        + dot(receiver_rows, w_first[pl.ds(2 * width, width)])
        + vectors[0]
    )
    sender_row = sender_ids[...].reshape(1, edges)
    inputs_t[pl.ds(0, width)] = jnp.transpose(edge[...])
    from_sender[...] = hot_columns(sender_row, table.shape[0])
    upstream[...] = dot(receiver_hot, cot[...])
    weight_sq[...] = slab_rows(jnp.square(w_first[...].astype(F32)), jnp.square(w_second[...].astype(F32)))
    wait_for(arriving, halo_sem)
    for i in range(edges // ROWS):
        rows = pl.ds(i * ROWS, ROWS)
        sender_rows = dot(from_sender[rows], table[...]).astype(BF16)
        inputs_t[pl.ds(width, width), rows] = jnp.transpose(sender_rows)
        pre = preact[rows] + dot(sender_rows, w_first[pl.ds(width, width)])
        sigma = 1.0 / (1.0 + jnp.exp(-pre))
        activation = (pre * sigma).astype(BF16)
        activation_t[:, rows] = jnp.transpose(activation)
        slope = sigma * (1.0 + pre * (1.0 - sigma))
        second_pre = dot(activation, w_second[...]) + vectors[1]
        centered = second_pre - jnp.mean(second_pre, -1, keepdims=True)
        variance = jnp.mean(centered * centered, -1, keepdims=True)
        inv_std = lax.rsqrt(variance + 1e-05)
        normalized = centered * inv_std
        scaled = upstream[rows] * vectors[2]
        back = (
            inv_std
            * (
                scaled
                - jnp.mean(scaled, -1, keepdims=True)
                - normalized * jnp.mean(scaled * normalized, -1, keepdims=True)
            )
        ).astype(BF16)
        norm_back[rows] = back
        pre_back[rows] = (dot_nt(back, w_second[...]) * slope).astype(BF16)

    other = 1 - c
    rings = (
        Ring(comm, "y", sent_a, from_core_a, own_a, staged_a, ring_a),
        Ring(comm, "z", sent_b, from_core_b, own_b, staged_b, ring_b),
    )
    cut, rest = first_out.shape[0], second_out.shape[0]
    for half, out_a, out_b in ((other, sent_a, sent_b), (c, own_a, own_b)):
        columns = pl.ds(pl.multiple_of(half * 256, 256), 256)
        split_blocks(dot(activation_t[...], norm_back[:, columns]), out_a, out_b, pl.ds(cut, rest))
        split_blocks(dot(inputs_t[...], pre_back[:, columns]), out_a, out_b, pl.ds(0, cut))
        if out_a is sent_a:
            for i in range(max(ny, nz)):
                for ring in rings:
                    order = offsets(ring.count) + [0]
                    if i < ring.count:
                        ring.pair(order[i], other)

    def table_part():
        sums = dot(hot_rows(sender_row, table.shape[0]), pre_back[...]).astype(BF16)
        grads = dot_nt(sums, w_first[pl.ds(width, width)])
        local_grad[...] = grads[:nodes]
        halo_grad[...] = grads[nodes:].astype(BF16).reshape(4, slots, width)

    def receiver_part():
        sums = dot(hot_rows(receiver_row, nodes), pre_back[...]).astype(BF16)
        local_grad[...] += dot_nt(sums, w_first[pl.ds(2 * width, width)]) + cot[...].astype(F32)

    stores = []

    def store(src, dst):
        copy = pltpu.make_async_copy(src, dst, store_sems.at[len(stores)])
        copy.start()
        stores.append(copy)

    def edge_part():
        edge_grad_out[...] = (upstream[...] + dot_nt(pre_back[...], w_first[pl.ds(0, width)])).astype(BF16)
        store(edge_grad_out, edge_grad_hbm)

    work = [table_part, receiver_part, edge_part]
    for step in range(max(nz, ny) // 2):
        for ring in rings:
            ring.step(step)
        if work:
            work.pop(0)()
    for part in work:
        part()
    rings[0].finish(over_a, over_sent_a)
    rings[1].finish(over_b, over_sent_b)
    to_z = scatter(comm, "z", lambda peer: over_sent_a.at[peer], cross_a)
    to_y = scatter(comm, "y", lambda peer: over_sent_b.at[peer], cross_b)
    share[0] = total_of(to_z, over_a[lax.axis_index("z")]).astype(BF16)
    share[1] = total_of(to_y, over_b[lax.axis_index("y")]).astype(BF16)
    here = lax.axis_index("x") * 2 + c
    shares[here] = share[...]
    group = comm.group(shares.at[pl.ds(0, 2 * across - 1)])
    copies = [comm.copy(group, share, shares.at[here], device) for device in narrow_peers()]
    for copy in copies:
        copy.wait_recv()
    slabs = []
    for core in (0, 1):
        for i in (0, 1):
            value = shares[core, i].astype(F32)
            for x in range(1, across):
                value = value + shares[2 * x + core, i].astype(F32)
            slabs.append(value)
    grads = jnp.concatenate(slabs, 1)
    square = grads * grads
    squares[0] = slab_rows(square[:cut], square[cut:])
    to_y = scatter(comm, "y", lambda peer: squares.at[0], squares_in.at[pl.ds(0, ny - 1)])
    back_sem, back_group = comm.recv_sem(), comm.group(halo_grad)
    for k, to in enumerate(
        (wide_neighbour(-1), wide_neighbour(1), narrow_neighbour(-1), narrow_neighbour(1))
    ):
        comm.copy(back_group, halo_grad.at[k], returned.at[k], to, back_sem)
    squares[1] = total_of(to_y, squares[0])
    to_z = scatter(comm, "z", lambda peer: squares.at[1], squares_in.at[pl.ds(ny - 1, nz - 1)])
    wait_for(returned, back_sem)
    node_grad_out[...] = (
        local_grad[...] + dot(hot_rows(send_row, nodes), returned[...].reshape(4 * slots, width))
    ).astype(BF16)
    store(node_grad_out, node_grad_hbm)
    grad_sq = total_of(to_z, squares[1])
    factors = [clip_rows(grad_sq, weight_sq[...], which) for which in (0, 1)]
    for i in range(4):
        columns = slice(128 * i, 128 * (i + 1))
        first = factors[0][2 * i : 2 * i + 1] * math.sqrt(cut * nz * ny)
        second = factors[1][2 * i + 1 : 2 * i + 2] * math.sqrt(rest * nz * ny)
        first_out[:, columns] = grads[:cut, columns] * first
        second_out[:, columns] = grads[cut:, columns] * second
    store(first_out, first_hbm)
    store(second_out, second_hbm)
    comm.drain()
    for copy in stores:
        copy.wait()


def deliver(*refs):
    count = (len(refs) - 2) // 3
    sources, targets, held = refs[:count], refs[count : 2 * count], refs[2 * count : 3 * count]
    moves = []
    for i in range(count):
        load = pltpu.make_async_copy(sources[i], held[i], refs[-2].at[i])
        load.start()
        moves.append((load, pltpu.make_async_copy(held[i], targets[i], refs[-1].at[i])))
    for load, store in moves:
        load.wait()
        store.start()
    for _, store in moves:
        store.wait()


def per_device(
    node_latent,
    edge_latent,
    node_cotangent,
    w_first,
    bias_first,
    w_second,
    bias_second,
    norm_gain,
    send_map,
    edge_sender,
    edge_receiver,
):
    nz, ny, across = lax.axis_size("z"), lax.axis_size("y"), lax.axis_size("x")
    nodes, width = node_latent.shape
    edges = edge_latent.shape[0]
    slots = send_map.shape[2]
    table_rows = nodes + 4 * slots
    first_rows, second_rows = w_first.shape[0] // (nz * ny), w_second.shape[0] // (nz * ny)
    rows = first_rows + second_rows
    hbm = pl.BlockSpec(memory_space=pltpu.HBM)
    copies = 1 + 3 * (ny + nz) - 4 + 2 + 2 * across - 1 + 3
    results = pl.pallas_call(
        kernel,
        out_shape=(
            jax.ShapeDtypeStruct((nodes, width), BF16),
            jax.ShapeDtypeStruct((edges, width), BF16),
            jax.ShapeDtypeStruct((first_rows, width), F32),
            jax.ShapeDtypeStruct((second_rows, width), F32),
        ),
        in_specs=[hbm] * 11,
        out_specs=(hbm,) * 4,
        scratch_shapes=[
            pltpu.VMEM(send_map.shape, jnp.int32),
            pltpu.VMEM((edges,), jnp.int32),
            pltpu.VMEM((edges,), jnp.int32),
            pltpu.VMEM((width,), BF16),
            pltpu.VMEM((width,), BF16),
            pltpu.VMEM((width,), BF16),
            pltpu.VMEM((table_rows, width), BF16),
            pltpu.VMEM((edges, width), BF16),
            pltpu.VMEM((nodes, width), BF16),
            pltpu.VMEM((3 * width, width), BF16),
            pltpu.VMEM((width, width), BF16),
            pltpu.VMEM((4, slots, width), BF16),
            pltpu.VMEM((3 * width, edges), BF16),
            pltpu.VMEM((edges, width), F32),
            pltpu.VMEM((edges, width), F32),
            pltpu.VMEM((width, edges), BF16),
            pltpu.VMEM((edges, width), BF16),
            pltpu.VMEM((edges, width), BF16),
            pltpu.VMEM((edges, table_rows), BF16),
            pltpu.VMEM((8, 128), F32),
            pltpu.VMEM((4, slots, width), BF16),
            pltpu.VMEM((4, slots, width), BF16),
            pltpu.VMEM((nodes, width), F32),
            pltpu.VMEM((ny, nz, rows, 128), BF16),
            pltpu.VMEM((nz, ny, rows, 128), BF16),
            pltpu.VMEM((ny, nz, rows, 128), BF16),
            pltpu.VMEM((nz, ny, rows, 128), BF16),
            pltpu.VMEM((ny, nz, rows, 128), F32),
            pltpu.VMEM((nz, ny, rows, 128), F32),
            pltpu.VMEM((2 * (ny - 1), nz // 2, rows, 128), BF16),
            pltpu.VMEM((2 * (nz - 1), ny // 2, rows, 128), BF16),
            pltpu.VMEM((2 * (ny - 1), nz // 2, rows, 128), BF16),
            pltpu.VMEM((2 * (nz - 1), ny // 2, rows, 128), BF16),
            pltpu.VMEM((nz, rows, 128), F32),
            pltpu.VMEM((ny, rows, 128), F32),
            pltpu.VMEM((nz, rows, 128), BF16),
            pltpu.VMEM((ny, rows, 128), BF16),
            pltpu.VMEM((nz - 1, rows, 128), BF16),
            pltpu.VMEM((ny - 1, rows, 128), BF16),
            pltpu.VMEM((2, rows, 128), BF16),
            pltpu.VMEM((2 * across, 2, rows, 128), BF16),
            pltpu.VMEM((2, 8, 128), F32),
            pltpu.VMEM((ny - 1 + nz - 1, 8, 128), F32),
            pltpu.VMEM((nodes, width), BF16),
            pltpu.VMEM((edges, width), BF16),
            pltpu.VMEM((first_rows, width), F32),
            pltpu.VMEM((second_rows, width), F32),
            pltpu.SemaphoreType.DMA((11,)),
            pltpu.SemaphoreType.DMA((4,)),
            pltpu.SemaphoreType.DMA((11,)),
            pltpu.SemaphoreType.DMA((copies,)),
        ],
        compiler_params=pltpu.CompilerParams(
            collective_id=0, has_side_effects=True, vmem_limit_bytes=56 << 20
        ),
    )(
        send_map,
        edge_sender,
        edge_receiver,
        bias_first,
        bias_second,
        norm_gain,
        node_latent,
        edge_latent,
        node_cotangent,
        w_first,
        w_second,
    )
    return pl.pallas_call(
        deliver,
        out_shape=[jax.ShapeDtypeStruct(v.shape, v.dtype) for v in results],
        in_specs=[hbm] * 4,
        out_specs=[hbm] * 4,
        scratch_shapes=[pltpu.VMEM(v.shape, v.dtype) for v in results]
        + [pltpu.SemaphoreType.DMA((4,))] * 2,
        compiler_params=pltpu.CompilerParams(vmem_limit_bytes=56 << 20),
    )(*results)


def solution(mesh):
    finer = Mesh(mesh.devices.reshape(8, 8, 4, 2), ALL)
    in_specs = (
        P(ALL, None),
        P(ALL, None),
        P(ALL, None),
        P(),
        P(),
        P(),
        P(),
        P(),
        P(ALL, None, None),
        P(ALL),
        P(ALL),
    )
    out_specs = (P(ALL, None), P(ALL, None), P(WIDE, None), P(WIDE, None))
    return jax.shard_map(
        per_device, mesh=finer, in_specs=in_specs, out_specs=out_specs, check_vma=False
    )
```

```python
import math

import jax
import jax.numpy as jnp
from jax import lax
from jax.experimental import pallas as pl
from jax.experimental.pallas import tpu as pltpu
from jax.sharding import Mesh
from jax.sharding import PartitionSpec as P

WIDE = ("z", "y")
ALL = ("z", "y", "x", "c")
MESH = pl.DeviceIdType.MESH
F32 = jnp.float32
BF16 = jnp.bfloat16
ROWS = 512


def dot(a, b):
    return jnp.dot(a, b, preferred_element_type=F32)


def dot_nt(a, b):
    return lax.dot_general(a, b, (((1,), (1,)), ((), ())), preferred_element_type=F32)


class Comm:
    def __init__(self, send_sems, recv_sems):
        self.send_sems, self.recv_sems, self.groups, self.used = send_sems, recv_sems, [], 0

    def group(self, sent):
        self.groups.append(sent)
        return len(self.groups) - 1

    def recv_sem(self):
        self.used += 1
        return self.recv_sems.at[self.used - 1]

    def copy(self, group, src, dst, to, recv_sem=None):
        copy = pltpu.make_async_remote_copy(
            src_ref=src,
            dst_ref=dst,
            send_sem=self.send_sems.at[group],
            recv_sem=self.recv_sem() if recv_sem is None else recv_sem,
            device_id=to,
            device_id_type=MESH,
        )
        copy.start()
        return copy

    def drain(self):
        for i, sent in enumerate(self.groups):
            wait_for(sent, self.send_sems.at[i])


def wait_for(ref, sem):
    pltpu.make_async_copy(ref, ref, sem).wait()


class Ring:
    def __init__(self, comm, axis, sent, paired, own, staged, slots):
        self.comm, self.axis, self.sent, self.paired, self.own = comm, axis, sent, paired, own
        self.count, self.me = lax.axis_size(axis), lax.axis_index(axis)
        self.half = own.shape[1] // 2
        self.chains = []
        used = 0
        for half in (0, 1):
            for sign in (-1, 1):
                hops = self.count // 2 - (0 if (sign < 0) == (half == 0) else 1)
                span = pl.ds(used, max(hops, 1))
                self.chains.append((half, sign, hops, staged.at[span], slots.at[span]))
                used += hops
        self.chains.sort(key=lambda chain: -chain[2])
        self.last = [None] * 4
        self.staged = staged
        self.pairs = {}
        self.pair_group = comm.group(sent)

    def at(self, offset):
        return lax.rem(self.me + offset + self.count, self.count)

    def pair(self, offset, other):
        owner = self.at(offset)
        self.pairs[offset % self.count] = self.comm.copy(
            self.pair_group, self.sent.at[owner], self.paired.at[owner], {"c": other}
        )

    def value(self, offset, half):
        pair = self.pairs.pop(offset % self.count, None)
        if pair is not None:
            pair.wait_recv()
        owner = self.at(offset)
        part = pl.ds(half * self.half, self.half)
        return self.own[owner, part] + self.paired[owner, part].astype(F32)

    def step(self, step):
        if step == 0:
            self.group = self.comm.group(self.staged)
        for i, (half, sign, hops, staged, slots) in enumerate(self.chains):
            if step >= hops:
                continue
            value = self.value(sign * (hops - step), half)
            if step:
                self.last[i].wait_recv()
                value = value + slots[step - 1].astype(F32)
            staged[step] = value.astype(BF16)
            self.last[i] = self.comm.copy(
                self.group, staged.at[step], slots.at[step], {self.axis: self.at(sign)}
            )

    def finish(self, over, over_sent):
        for half in (0, 1):
            value = self.value(0, half)
            for i, (chain_half, _, hops, _, slots) in enumerate(self.chains):
                if chain_half == half and hops:
                    self.last[i].wait_recv()
                    value = value + slots[hops - 1].astype(F32)
            part = pl.ds(half * self.half, self.half)
            over[part] = value
            over_sent[part] = value.astype(BF16)


def offsets(count):
    return sorted(range(1, count), key=lambda k: -min(k, count - k))


def scatter(comm, axis, parts, slots):
    count, me = lax.axis_size(axis), lax.axis_index(axis)
    sem, group = comm.recv_sem(), comm.group(slots)
    for k in offsets(count):
        peer = lax.rem(me + k, count)
        comm.copy(group, parts(peer), slots.at[k - 1], {axis: peer}, sem)
    return slots, sem


def total_of(arriving, own):
    slots, sem = arriving
    wait_for(slots, sem)
    value = own
    for k in range(slots.shape[0]):
        value = value + slots[k].astype(F32)
    return value


def narrow_peers():
    across, cores = lax.axis_size("x"), lax.axis_size("c")
    x, c = lax.axis_index("x"), lax.axis_index("c")
    steps = offsets(across) + [0]
    return [
        {"x": lax.rem(x + i, across), "c": lax.rem(c + j, cores)}
        for i in steps
        for j in range(cores)
        if i or j
    ]


def wide_neighbour(step):
    nz, ny = lax.axis_size("z"), lax.axis_size("y")
    index = lax.rem(lax.axis_index("z") * ny + lax.axis_index("y") + step + nz * ny, nz * ny)
    return {"z": index // ny, "y": lax.rem(index, ny)}


def narrow_neighbour(step):
    across, cores = lax.axis_size("x"), lax.axis_size("c")
    count = across * cores
    index = lax.rem(lax.axis_index("x") * cores + lax.axis_index("c") + step + count, count)
    return {"x": index // cores, "c": lax.rem(index, cores)}


def greeted():
    found = [wide_neighbour(1), wide_neighbour(-1)]
    for axis in ("z", "y"):
        count, me = lax.axis_size(axis), lax.axis_index(axis)
        found += [{axis: lax.rem(me + k, count)} for k in sorted({1, count - 1})]
    return found + narrow_peers()


def as_columns(row):
    blocks = [
        jnp.transpose(jnp.broadcast_to(row[:, 128 * i : 128 * (i + 1)], (128, 128)))
        for i in range(row.shape[1] // 128)
    ]
    return jnp.concatenate(blocks, 0)


def hot_rows(row, count):
    ids = lax.broadcasted_iota(jnp.int32, (count, row.shape[1]), 0)
    return jnp.where(ids == row, 1.0, 0.0).astype(BF16)


def hot_columns(row, count):
    columns = as_columns(row)
    ids = lax.broadcasted_iota(jnp.int32, columns.shape, 1)
    blocks = [jnp.where(columns == ids + 128 * i, 1.0, 0.0) for i in range(count // 128)]
    return jnp.concatenate(blocks, 1).astype(BF16)


def clip_rows(grad_sq, weight_sq, which):
    ratio = jnp.sqrt((grad_sq + 1e-06) / (weight_sq + 1e-06))
    rows = lax.broadcasted_iota(jnp.int32, ratio.shape, 0)
    mine = lax.rem(rows, 2) == which
    mean_ratio = jnp.sum(jnp.where(mine, ratio, 0.0)) / (ratio.shape[0] // 2 * ratio.shape[1])
    return jnp.minimum(1.0 / (mean_ratio * jnp.sqrt(weight_sq + 1e-06)), 1.0 / jnp.sqrt(grad_sq + 1e-06))


def slab_rows(first, second):
    rows = []
    for i in range(4):
        columns = slice(128 * i, 128 * (i + 1))
        rows += [
            jnp.sum(first[:, columns], 0, keepdims=True),
            jnp.sum(second[:, columns], 0, keepdims=True),
        ]
    return jnp.concatenate(rows, 0)


def split_blocks(value, out_a, out_b, rows):
    ny, nz = out_a.shape[:2]
    height = value.shape[0] // (ny * nz)
    lower = value[:, :128].reshape(nz, ny, height, 128)
    for y in range(ny):
        out_a[y, :, rows, :] = lower[:, y].astype(out_a.dtype)
    out_b[:, :, rows, :] = value[:, 128:].reshape(nz, ny, height, 128).astype(out_b.dtype)


def kernel(
    send_hbm,
    sender_hbm,
    receiver_hbm,
    bias_first_hbm,
    bias_second_hbm,
    gain_hbm,
    node_hbm,
    edge_hbm,
    cot_hbm,
    w_first_hbm,
    w_second_hbm,
    node_grad_hbm,
    edge_grad_hbm,
    first_hbm,
    second_hbm,
    send_map,
    sender_ids,
    receiver_ids,
    bias_first,
    bias_second,
    norm_gain,
    table,
    edge,
    cot,
    w_first,
    w_second,
    outgoing,
    inputs_t,
    preact,
    upstream,
    activation_t,
    norm_back,
    pre_back,
    from_sender,
    scaled_mean,
    local_rows,
    weight_sq,
    halo_grad,
    returned,
    local_grad,
    sent_a,
    sent_b,
    from_core_a,
    from_core_b,
    own_a,
    own_b,
    staged_a,
    staged_b,
    ring_a,
    ring_b,
    over_a,
    over_b,
    over_sent_a,
    over_sent_b,
    cross_a,
    cross_b,
    share,
    shares,
    squares,
    squares_in,
    node_grad_out,
    edge_grad_out,
    first_out,
    second_out,
    load_sems,
    store_sems,
    send_sems,
    recv_sems,
):
    comm = Comm(send_sems, recv_sems)
    c = lax.axis_index("c")
    nz, ny, across = lax.axis_size("z"), lax.axis_size("y"), lax.axis_size("x")
    nodes, width = node_hbm.shape
    edges = edge_hbm.shape[0]
    slots = outgoing.shape[1]
    barrier = pltpu.get_barrier_semaphore()
    peers = greeted()
    for peer in peers:
        pl.semaphore_signal(barrier, 1, device_id=peer, device_id_type=MESH)
    loads = [
        pltpu.make_async_copy(src, dst, load_sems.at[i])
        for i, (src, dst) in enumerate(
            (
                (send_hbm, send_map),
                (node_hbm, table.at[pl.ds(0, nodes)]),
                (receiver_hbm, receiver_ids),
                (edge_hbm, edge),
                (w_first_hbm, w_first),
                (bias_first_hbm, bias_first),
                (sender_hbm, sender_ids),
                (cot_hbm, cot),
                (w_second_hbm, w_second),
                (bias_second_hbm, bias_second),
                (gain_hbm, norm_gain),
            )
        )
    ]
    for load in loads:
        load.start()
    loads[0].wait()
    send_row = jnp.concatenate([send_map[0, k : k + 1, :] for k in range(4)], 1)
    send_hot = hot_columns(send_row, nodes)
    loads[1].wait()
    node = table[pl.ds(0, nodes)]
    outgoing[...] = dot(send_hot, node).astype(BF16).reshape(4, slots, width)
    pl.semaphore_wait(barrier, len(peers))
    halo_sem, halo_group = comm.recv_sem(), comm.group(outgoing)
    arriving = table.at[pl.ds(nodes, 4 * slots)]
    for k, to in enumerate(
        (wide_neighbour(1), wide_neighbour(-1), narrow_neighbour(1), narrow_neighbour(-1))
    ):
        comm.copy(halo_group, outgoing.at[k], table.at[pl.ds(nodes + k * slots, slots)], to, halo_sem)
    loads[2].wait()
    receiver_row = receiver_ids[...].reshape(1, edges)
    receiver_hot = hot_columns(receiver_row, nodes)
    receiver_rows = dot(receiver_hot, node).astype(BF16)
    inputs_t[pl.ds(2 * width, width)] = jnp.transpose(receiver_rows)
    for load in loads[3:]:
        load.wait()
    vectors = [v[...].astype(F32).reshape(1, width) for v in (bias_first, bias_second, norm_gain)]
    preact[...] = (
        dot(edge[...], w_first[pl.ds(0, width)])
        + dot(receiver_rows, w_first[pl.ds(2 * width, width)])
        + vectors[0]
    )
    sender_row = sender_ids[...].reshape(1, edges)
    inputs_t[pl.ds(0, width)] = jnp.transpose(edge[...])
    from_sender[...] = hot_columns(sender_row, table.shape[0])
    upstream[...] = dot(receiver_hot, cot[...])
    scaled_mean[...] = jnp.mean(upstream[...] * vectors[2], -1, keepdims=True)
    local_rows[...] = dot(from_sender[:, pl.ds(0, nodes)], node).astype(BF16)
    preact[...] += dot(local_rows[...], w_first[pl.ds(width, width)])
    weight_sq[...] = slab_rows(jnp.square(w_first[...].astype(F32)), jnp.square(w_second[...].astype(F32)))
    wait_for(arriving, halo_sem)
    for i in range(edges // ROWS):
        rows = pl.ds(i * ROWS, ROWS)
        halo_rows = dot(from_sender[rows, pl.ds(nodes, 4 * slots)], arriving[...]).astype(BF16)
        inputs_t[pl.ds(width, width), rows] = jnp.transpose(local_rows[rows] + halo_rows)
        pre = preact[rows] + dot(halo_rows, w_first[pl.ds(width, width)])
        sigma = 0.5 * jnp.tanh(0.5 * pre) + 0.5
        activation = (pre * sigma).astype(BF16)
        activation_t[:, rows] = jnp.transpose(activation)
        slope = sigma * (1.0 + pre * (1.0 - sigma))
        second_pre = dot(activation, w_second[...]) + vectors[1]
        centered = second_pre - jnp.mean(second_pre, -1, keepdims=True)
        variance = jnp.mean(centered * centered, -1, keepdims=True)
        inv_std = lax.rsqrt(variance + 1e-05)
        normalized = centered * inv_std
        scaled = upstream[rows] * vectors[2]
        back = (
            inv_std
            * (
                scaled
                - scaled_mean[rows]
                - normalized * jnp.mean(scaled * normalized, -1, keepdims=True)
            )
        ).astype(BF16)
        norm_back[rows] = back
        pre_back[rows] = (dot_nt(back, w_second[...]) * slope).astype(BF16)

    other = 1 - c
    rings = (
        Ring(comm, "y", sent_a, from_core_a, own_a, staged_a, ring_a),
        Ring(comm, "z", sent_b, from_core_b, own_b, staged_b, ring_b),
    )
    cut, rest = first_out.shape[0], second_out.shape[0]
    for half, out_a, out_b in ((other, sent_a, sent_b), (c, own_a, own_b)):
        columns = pl.ds(pl.multiple_of(half * 256, 256), 256)
        split_blocks(dot(activation_t[...], norm_back[:, columns]), out_a, out_b, pl.ds(cut, rest))
        split_blocks(dot(inputs_t[...], pre_back[:, columns]), out_a, out_b, pl.ds(0, cut))
        if out_a is sent_a:
            for i in range(max(ny, nz)):
                for ring in rings:
                    order = offsets(ring.count) + [0]
                    if i < ring.count:
                        ring.pair(order[i], other)

    def table_part():
        sums = dot(hot_rows(sender_row, table.shape[0]), pre_back[...]).astype(BF16)
        grads = dot_nt(sums, w_first[pl.ds(width, width)])
        local_grad[...] = grads[:nodes]
        halo_grad[...] = grads[nodes:].astype(BF16).reshape(4, slots, width)

    def receiver_part():
        sums = dot(hot_rows(receiver_row, nodes), pre_back[...]).astype(BF16)
        local_grad[...] += dot_nt(sums, w_first[pl.ds(2 * width, width)]) + cot[...].astype(F32)

    stores = []

    def store(src, dst):
        copy = pltpu.make_async_copy(src, dst, store_sems.at[len(stores)])
        copy.start()
        stores.append(copy)

    def edge_part():
        edge_grad_out[...] = (upstream[...] + dot_nt(pre_back[...], w_first[pl.ds(0, width)])).astype(BF16)
        store(edge_grad_out, edge_grad_hbm)

    work = [table_part, receiver_part, edge_part]
    for step in range(max(nz, ny) // 2):
        for ring in rings:
            ring.step(step)
        if work:
            work.pop(0)()
    for part in work:
        part()
    rings[0].finish(over_a, over_sent_a)
    rings[1].finish(over_b, over_sent_b)
    to_z = scatter(comm, "z", lambda peer: over_sent_a.at[peer], cross_a)
    to_y = scatter(comm, "y", lambda peer: over_sent_b.at[peer], cross_b)
    share[0] = total_of(to_z, over_a[lax.axis_index("z")]).astype(BF16)
    share[1] = total_of(to_y, over_b[lax.axis_index("y")]).astype(BF16)
    here = lax.axis_index("x") * 2 + c
    shares[here] = share[...]
    group = comm.group(shares.at[pl.ds(0, 2 * across - 1)])
    copies = [comm.copy(group, share, shares.at[here], device) for device in narrow_peers()]
    for copy in copies:
        copy.wait_recv()
    slabs = []
    for core in (0, 1):
        for i in (0, 1):
            value = shares[core, i].astype(F32)
            for x in range(1, across):
                value = value + shares[2 * x + core, i].astype(F32)
            slabs.append(value)
    grads = jnp.concatenate(slabs, 1)
    square = grads * grads
    squares[0] = slab_rows(square[:cut], square[cut:])
    to_y = scatter(comm, "y", lambda peer: squares.at[0], squares_in.at[pl.ds(0, ny - 1)])
    back_sem, back_group = comm.recv_sem(), comm.group(halo_grad)
    for k, to in enumerate(
        (wide_neighbour(-1), wide_neighbour(1), narrow_neighbour(-1), narrow_neighbour(1))
    ):
        comm.copy(back_group, halo_grad.at[k], returned.at[k], to, back_sem)
    squares[1] = total_of(to_y, squares[0])
    to_z = scatter(comm, "z", lambda peer: squares.at[1], squares_in.at[pl.ds(ny - 1, nz - 1)])
    wait_for(returned, back_sem)
    node_grad_out[...] = (
        local_grad[...] + dot(hot_rows(send_row, nodes), returned[...].reshape(4 * slots, width))
    ).astype(BF16)
    store(node_grad_out, node_grad_hbm)
    grad_sq = total_of(to_z, squares[1])
    factors = [clip_rows(grad_sq, weight_sq[...], which) for which in (0, 1)]
    for i in range(4):
        columns = slice(128 * i, 128 * (i + 1))
        first = factors[0][2 * i : 2 * i + 1] * math.sqrt(cut * nz * ny)
        second = factors[1][2 * i + 1 : 2 * i + 2] * math.sqrt(rest * nz * ny)
        first_out[:, columns] = grads[:cut, columns] * first
        second_out[:, columns] = grads[cut:, columns] * second
    store(first_out, first_hbm)
    store(second_out, second_hbm)
    comm.drain()
    for copy in stores:
        copy.wait()


def deliver(*refs):
    count = (len(refs) - 2) // 3
    moves = []
    for i in sorted(range(count), key=lambda i: -refs[i].shape[0]):
        source, target, held = refs[i], refs[count + i], refs[2 * count + i]
        height = min(128, source.shape[0])
        for j in range(source.shape[0] // height):
            rows, k = pl.ds(j * height, height), len(moves)
            load = pltpu.make_async_copy(source.at[rows], held.at[rows], refs[-2].at[k])
            load.start()
            moves.append((load, pltpu.make_async_copy(held.at[rows], target.at[rows], refs[-1].at[k])))
    for load, store in moves:
        load.wait()
        store.start()
    for _, store in moves:
        store.wait()


def per_device(
    node_latent,
    edge_latent,
    node_cotangent,
    w_first,
    bias_first,
    w_second,
    bias_second,
    norm_gain,
    send_map,
    edge_sender,
    edge_receiver,
):
    nz, ny, across = lax.axis_size("z"), lax.axis_size("y"), lax.axis_size("x")
    nodes, width = node_latent.shape
    edges = edge_latent.shape[0]
    slots = send_map.shape[2]
    table_rows = nodes + 4 * slots
    first_rows, second_rows = w_first.shape[0] // (nz * ny), w_second.shape[0] // (nz * ny)
    rows = first_rows + second_rows
    hbm = pl.BlockSpec(memory_space=pltpu.HBM)
    copies = 1 + 3 * (ny + nz) - 4 + 2 + 2 * across - 1 + 3
    results = pl.pallas_call(
        kernel,
        out_shape=(
            jax.ShapeDtypeStruct((nodes, width), BF16),
            jax.ShapeDtypeStruct((edges, width), BF16),
            jax.ShapeDtypeStruct((first_rows, width), F32),
            jax.ShapeDtypeStruct((second_rows, width), F32),
        ),
        in_specs=[hbm] * 11,
        out_specs=(hbm,) * 4,
        scratch_shapes=[
            pltpu.VMEM(send_map.shape, jnp.int32),
            pltpu.VMEM((edges,), jnp.int32),
            pltpu.VMEM((edges,), jnp.int32),
            pltpu.VMEM((width,), BF16),
            pltpu.VMEM((width,), BF16),
            pltpu.VMEM((width,), BF16),
            pltpu.VMEM((table_rows, width), BF16),
            pltpu.VMEM((edges, width), BF16),
            pltpu.VMEM((nodes, width), BF16),
            pltpu.VMEM((3 * width, width), BF16),
            pltpu.VMEM((width, width), BF16),
            pltpu.VMEM((4, slots, width), BF16),
            pltpu.VMEM((3 * width, edges), BF16),
            pltpu.VMEM((edges, width), F32),
            pltpu.VMEM((edges, width), F32),
            pltpu.VMEM((width, edges), BF16),
            pltpu.VMEM((edges, width), BF16),
            pltpu.VMEM((edges, width), BF16),
            pltpu.VMEM((edges, table_rows), BF16),
            pltpu.VMEM((edges, 1), F32),
            pltpu.VMEM((edges, width), BF16),
            pltpu.VMEM((8, 128), F32),
            pltpu.VMEM((4, slots, width), BF16),
            pltpu.VMEM((4, slots, width), BF16),
            pltpu.VMEM((nodes, width), F32),
            pltpu.VMEM((ny, nz, rows, 128), BF16),
            pltpu.VMEM((nz, ny, rows, 128), BF16),
            pltpu.VMEM((ny, nz, rows, 128), BF16),
            pltpu.VMEM((nz, ny, rows, 128), BF16),
            pltpu.VMEM((ny, nz, rows, 128), F32),
            pltpu.VMEM((nz, ny, rows, 128), F32),
            pltpu.VMEM((2 * (ny - 1), nz // 2, rows, 128), BF16),
            pltpu.VMEM((2 * (nz - 1), ny // 2, rows, 128), BF16),
            pltpu.VMEM((2 * (ny - 1), nz // 2, rows, 128), BF16),
            pltpu.VMEM((2 * (nz - 1), ny // 2, rows, 128), BF16),
            pltpu.VMEM((nz, rows, 128), F32),
            pltpu.VMEM((ny, rows, 128), F32),
            pltpu.VMEM((nz, rows, 128), BF16),
            pltpu.VMEM((ny, rows, 128), BF16),
            pltpu.VMEM((nz - 1, rows, 128), BF16),
            pltpu.VMEM((ny - 1, rows, 128), BF16),
            pltpu.VMEM((2, rows, 128), BF16),
            pltpu.VMEM((2 * across, 2, rows, 128), BF16),
            pltpu.VMEM((2, 8, 128), F32),
            pltpu.VMEM((ny - 1 + nz - 1, 8, 128), F32),
            pltpu.VMEM((nodes, width), BF16),
            pltpu.VMEM((edges, width), BF16),
            pltpu.VMEM((first_rows, width), F32),
            pltpu.VMEM((second_rows, width), F32),
            pltpu.SemaphoreType.DMA((11,)),
            pltpu.SemaphoreType.DMA((4,)),
            pltpu.SemaphoreType.DMA((11,)),
            pltpu.SemaphoreType.DMA((copies,)),
        ],
        compiler_params=pltpu.CompilerParams(
            collective_id=0, has_side_effects=True, vmem_limit_bytes=56 << 20
        ),
    )(
        send_map,
        edge_sender,
        edge_receiver,
        bias_first,
        bias_second,
        norm_gain,
        node_latent,
        edge_latent,
        node_cotangent,
        w_first,
        w_second,
    )
    return pl.pallas_call(
        deliver,
        out_shape=[jax.ShapeDtypeStruct(v.shape, v.dtype) for v in results],
        in_specs=[hbm] * 4,
        out_specs=[hbm] * 4,
        scratch_shapes=[pltpu.VMEM(v.shape, v.dtype) for v in results]
        + [pltpu.SemaphoreType.DMA((7,))] * 2,
        compiler_params=pltpu.CompilerParams(vmem_limit_bytes=56 << 20),
    )(*results)


def solution(mesh):
    finer = Mesh(mesh.devices.reshape(8, 8, 4, 2), ALL)
    in_specs = (
        P(ALL, None),
        P(ALL, None),
        P(ALL, None),
        P(),
        P(),
        P(),
        P(),
        P(),
        P(ALL, None, None),
        P(ALL),
        P(ALL),
    )
    out_specs = (P(ALL, None), P(ALL, None), P(WIDE, None), P(WIDE, None))
    return jax.shard_map(
        per_device, mesh=finer, in_specs=in_specs, out_specs=out_specs, check_vma=False
    )
```

```python
import math

import jax
import jax.numpy as jnp
from jax import lax
from jax.experimental import pallas as pl
from jax.experimental.pallas import tpu as pltpu
from jax.sharding import Mesh
from jax.sharding import PartitionSpec as P

WIDE = ("z", "y")
ALL = ("z", "y", "x", "c")
MESH = pl.DeviceIdType.MESH
F32 = jnp.float32
BF16 = jnp.bfloat16
ROWS = 512


def dot(a, b):
    return jnp.dot(a, b, preferred_element_type=F32)


def dot_nt(a, b):
    return lax.dot_general(a, b, (((1,), (1,)), ((), ())), preferred_element_type=F32)


class Comm:
    def __init__(self, send_sems, recv_sems):
        self.send_sems, self.recv_sems, self.groups, self.used = send_sems, recv_sems, [], 0

    def group(self, sent):
        self.groups.append(sent)
        return len(self.groups) - 1

    def recv_sem(self):
        self.used += 1
        return self.recv_sems.at[self.used - 1]

    def copy(self, group, src, dst, to, recv_sem=None):
        copy = pltpu.make_async_remote_copy(
            src_ref=src,
            dst_ref=dst,
            send_sem=self.send_sems.at[group],
            recv_sem=self.recv_sem() if recv_sem is None else recv_sem,
            device_id=to,
            device_id_type=MESH,
        )
        copy.start()
        return copy

    def drain(self):
        for i, sent in enumerate(self.groups):
            wait_for(sent, self.send_sems.at[i])


def wait_for(ref, sem):
    pltpu.make_async_copy(ref, ref, sem).wait()


class Ring:
    def __init__(self, comm, axis, sent, paired, own, staged, slots):
        self.comm, self.axis, self.sent, self.paired, self.own = comm, axis, sent, paired, own
        self.count, self.me = lax.axis_size(axis), lax.axis_index(axis)
        self.half = own.shape[1] // 2
        self.chains = []
        used = 0
        for half in (0, 1):
            for sign in (-1, 1):
                hops = self.count // 2 - (0 if (sign < 0) == (half == 0) else 1)
                span = pl.ds(used, max(hops, 1))
                self.chains.append((half, sign, hops, staged.at[span], slots.at[span]))
                used += hops
        self.chains.sort(key=lambda chain: -chain[2])
        self.last = [None] * 4
        self.staged = staged
        self.pairs = {}
        self.pair_group = comm.group(sent)

    def at(self, offset):
        return lax.rem(self.me + offset + self.count, self.count)

    def pair(self, offset, other):
        owner = self.at(offset)
        self.pairs[offset % self.count] = self.comm.copy(
            self.pair_group, self.sent.at[owner], self.paired.at[owner], {"c": other}
        )

    def value(self, offset, half):
        pair = self.pairs.pop(offset % self.count, None)
        if pair is not None:
            pair.wait_recv()
        owner = self.at(offset)
        part = pl.ds(half * self.half, self.half)
        return self.own[owner, part] + self.paired[owner, part].astype(F32)

    def step(self, step):
        if step == 0:
            self.group = self.comm.group(self.staged)
        for i, (half, sign, hops, staged, slots) in enumerate(self.chains):
            if step >= hops:
                continue
            value = self.value(sign * (hops - step), half)
            if step:
                self.last[i].wait_recv()
                value = value + slots[step - 1].astype(F32)
            staged[step] = value.astype(BF16)
            self.last[i] = self.comm.copy(
                self.group, staged.at[step], slots.at[step], {self.axis: self.at(sign)}
            )

    def finish(self, over, over_sent):
        for half in (0, 1):
            value = self.value(0, half)
            for i, (chain_half, _, hops, _, slots) in enumerate(self.chains):
                if chain_half == half and hops:
                    self.last[i].wait_recv()
                    value = value + slots[hops - 1].astype(F32)
            part = pl.ds(half * self.half, self.half)
            over[part] = value
            over_sent[part] = value.astype(BF16)


def offsets(count):
    return sorted(range(1, count), key=lambda k: -min(k, count - k))


def scatter(comm, axis, parts, slots):
    count, me = lax.axis_size(axis), lax.axis_index(axis)
    sem, group = comm.recv_sem(), comm.group(slots)
    for k in offsets(count):
        peer = lax.rem(me + k, count)
        comm.copy(group, parts(peer), slots.at[k - 1], {axis: peer}, sem)
    return slots, sem


def total_of(arriving, own):
    slots, sem = arriving
    wait_for(slots, sem)
    value = own
    for k in range(slots.shape[0]):
        value = value + slots[k].astype(F32)
    return value


def narrow_peers():
    across, cores = lax.axis_size("x"), lax.axis_size("c")
    x, c = lax.axis_index("x"), lax.axis_index("c")
    steps = offsets(across) + [0]
    return [
        {"x": lax.rem(x + i, across), "c": lax.rem(c + j, cores)}
        for i in steps
        for j in range(cores)
        if i or j
    ]


def wide_neighbour(step):
    nz, ny = lax.axis_size("z"), lax.axis_size("y")
    index = lax.rem(lax.axis_index("z") * ny + lax.axis_index("y") + step + nz * ny, nz * ny)
    return {"z": index // ny, "y": lax.rem(index, ny)}


def narrow_neighbour(step):
    across, cores = lax.axis_size("x"), lax.axis_size("c")
    count = across * cores
    index = lax.rem(lax.axis_index("x") * cores + lax.axis_index("c") + step + count, count)
    return {"x": index // cores, "c": lax.rem(index, cores)}


def greeted():
    found = [wide_neighbour(1), wide_neighbour(-1)]
    for axis in ("z", "y"):
        count, me = lax.axis_size(axis), lax.axis_index(axis)
        found += [{axis: lax.rem(me + k, count)} for k in sorted({1, count - 1})]
    return found + narrow_peers()


def as_columns(row):
    blocks = [
        jnp.transpose(jnp.broadcast_to(row[:, 128 * i : 128 * (i + 1)], (128, 128)))
        for i in range(row.shape[1] // 128)
    ]
    return jnp.concatenate(blocks, 0)


def hot_rows(row, count):
    ids = lax.broadcasted_iota(jnp.int32, (count, row.shape[1]), 0)
    return jnp.where(ids == row, 1.0, 0.0).astype(BF16)


def hot_columns(row, count):
    columns = as_columns(row)
    ids = lax.broadcasted_iota(jnp.int32, columns.shape, 1)
    blocks = [jnp.where(columns == ids + 128 * i, 1.0, 0.0) for i in range(count // 128)]
    return jnp.concatenate(blocks, 1).astype(BF16)


def clip_rows(grad_sq, weight_sq, which):
    ratio = jnp.sqrt((grad_sq + 1e-06) / (weight_sq + 1e-06))
    rows = lax.broadcasted_iota(jnp.int32, ratio.shape, 0)
    mine = lax.rem(rows, 2) == which
    mean_ratio = jnp.sum(jnp.where(mine, ratio, 0.0)) / (ratio.shape[0] // 2 * ratio.shape[1])
    return jnp.minimum(1.0 / (mean_ratio * jnp.sqrt(weight_sq + 1e-06)), 1.0 / jnp.sqrt(grad_sq + 1e-06))


def slab_rows(first, second):
    rows = []
    for i in range(4):
        columns = slice(128 * i, 128 * (i + 1))
        rows += [
            jnp.sum(first[:, columns], 0, keepdims=True),
            jnp.sum(second[:, columns], 0, keepdims=True),
        ]
    return jnp.concatenate(rows, 0)


def split_blocks(value, out_a, out_b, rows):
    ny, nz = out_a.shape[:2]
    height = value.shape[0] // (ny * nz)
    lower = value[:, :128].reshape(nz, ny, height, 128)
    for y in range(ny):
        out_a[y, :, rows, :] = lower[:, y].astype(out_a.dtype)
    out_b[:, :, rows, :] = value[:, 128:].reshape(nz, ny, height, 128).astype(out_b.dtype)


def kernel(
    send_hbm,
    sender_hbm,
    receiver_hbm,
    bias_first_hbm,
    bias_second_hbm,
    gain_hbm,
    node_hbm,
    edge_hbm,
    cot_hbm,
    w_first_hbm,
    w_second_hbm,
    node_grad_hbm,
    edge_grad_hbm,
    first_hbm,
    second_hbm,
    send_map,
    sender_ids,
    receiver_ids,
    bias_first,
    bias_second,
    norm_gain,
    table,
    edge,
    cot,
    w_first,
    w_second,
    outgoing,
    inputs_t,
    preact,
    upstream,
    activation_t,
    norm_back,
    pre_back,
    from_sender,
    scaled_mean,
    local_rows,
    weight_sq,
    halo_grad,
    returned,
    local_grad,
    sent_a,
    sent_b,
    from_core_a,
    from_core_b,
    own_a,
    own_b,
    staged_a,
    staged_b,
    ring_a,
    ring_b,
    over_a,
    over_b,
    over_sent_a,
    over_sent_b,
    cross_a,
    cross_b,
    share,
    shares,
    squares,
    squares_in,
    node_grad_out,
    edge_grad_out,
    first_out,
    second_out,
    load_sems,
    store_sems,
    send_sems,
    recv_sems,
):
    comm = Comm(send_sems, recv_sems)
    c = lax.axis_index("c")
    nz, ny, across = lax.axis_size("z"), lax.axis_size("y"), lax.axis_size("x")
    nodes, width = node_hbm.shape
    edges = edge_hbm.shape[0]
    slots = outgoing.shape[1]
    barrier = pltpu.get_barrier_semaphore()
    peers = greeted()
    for peer in peers:
        pl.semaphore_signal(barrier, 1, device_id=peer, device_id_type=MESH)
    loads = [
        pltpu.make_async_copy(src, dst, load_sems.at[i])
        for i, (src, dst) in enumerate(
            (
                (send_hbm, send_map),
                (node_hbm, table.at[pl.ds(0, nodes)]),
                (receiver_hbm, receiver_ids),
                (edge_hbm, edge),
                (w_first_hbm, w_first),
                (bias_first_hbm, bias_first),
                (sender_hbm, sender_ids),
                (cot_hbm, cot),
                (w_second_hbm, w_second),
                (bias_second_hbm, bias_second),
                (gain_hbm, norm_gain),
            )
        )
    ]
    for load in loads:
        load.start()
    loads[0].wait()
    send_row = jnp.concatenate([send_map[0, k : k + 1, :] for k in range(4)], 1)
    send_hot = hot_columns(send_row, nodes)
    loads[1].wait()
    node = table[pl.ds(0, nodes)]
    outgoing[...] = dot(send_hot, node).astype(BF16).reshape(4, slots, width)
    pl.semaphore_wait(barrier, len(peers))
    halo_sem, halo_group = comm.recv_sem(), comm.group(outgoing)
    arriving = table.at[pl.ds(nodes, 4 * slots)]
    for k, to in enumerate(
        (wide_neighbour(1), wide_neighbour(-1), narrow_neighbour(1), narrow_neighbour(-1))
    ):
        comm.copy(halo_group, outgoing.at[k], table.at[pl.ds(nodes + k * slots, slots)], to, halo_sem)
    loads[2].wait()
    receiver_row = receiver_ids[...].reshape(1, edges)
    receiver_hot = hot_columns(receiver_row, nodes)
    receiver_rows = dot(receiver_hot, node).astype(BF16)
    inputs_t[pl.ds(2 * width, width)] = jnp.transpose(receiver_rows)
    for load in loads[3:]:
        load.wait()
    vectors = [v[...].astype(F32).reshape(1, width) for v in (bias_first, bias_second, norm_gain)]
    preact[...] = (
        dot(edge[...], w_first[pl.ds(0, width)])
        + dot(receiver_rows, w_first[pl.ds(2 * width, width)])
        + vectors[0]
    )
    sender_row = sender_ids[...].reshape(1, edges)
    inputs_t[pl.ds(0, width)] = jnp.transpose(edge[...])
    from_sender[...] = hot_columns(sender_row, table.shape[0])
    upstream[...] = dot(receiver_hot, cot[...])
    scaled_mean[...] = jnp.mean(upstream[...] * vectors[2], -1, keepdims=True)
    local_rows[...] = dot(from_sender[:, pl.ds(0, nodes)], node).astype(BF16)
    preact[...] += dot(local_rows[...], w_first[pl.ds(width, width)])
    weight_sq[...] = slab_rows(jnp.square(w_first[...].astype(F32)), jnp.square(w_second[...].astype(F32)))
    wait_for(arriving, halo_sem)
    for i in range(edges // ROWS):
        rows = pl.ds(i * ROWS, ROWS)
        halo_rows = dot(from_sender[rows, pl.ds(nodes, 4 * slots)], arriving[...]).astype(BF16)
        inputs_t[pl.ds(width, width), rows] = jnp.transpose(local_rows[rows] + halo_rows)
        pre = preact[rows] + dot(halo_rows, w_first[pl.ds(width, width)])
        sigma = 0.5 * jnp.tanh(0.5 * pre) + 0.5
        activation = (pre * sigma).astype(BF16)
        activation_t[:, rows] = jnp.transpose(activation)
        slope = sigma * (1.0 + pre * (1.0 - sigma))
        second_pre = dot(activation, w_second[...]) + vectors[1]
        centered = second_pre - jnp.mean(second_pre, -1, keepdims=True)
        variance = jnp.mean(centered * centered, -1, keepdims=True)
        inv_std = lax.rsqrt(variance + 1e-05)
        normalized = centered * inv_std
        scaled = upstream[rows] * vectors[2]
        back = (
            inv_std
            * (
                scaled
                - scaled_mean[rows]
                - normalized * jnp.mean(scaled * normalized, -1, keepdims=True)
            )
        ).astype(BF16)
        norm_back[rows] = back
        pre_back[rows] = (dot_nt(back, w_second[...]) * slope).astype(BF16)

    other = 1 - c
    rings = (
        Ring(comm, "y", sent_a, from_core_a, own_a, staged_a, ring_a),
        Ring(comm, "z", sent_b, from_core_b, own_b, staged_b, ring_b),
    )
    cut, rest = first_out.shape[0], second_out.shape[0]
    for half, out_a, out_b in ((other, sent_a, sent_b), (c, own_a, own_b)):
        columns = pl.ds(pl.multiple_of(half * 256, 256), 256)
        split_blocks(dot(activation_t[...], norm_back[:, columns]), out_a, out_b, pl.ds(cut, rest))
        split_blocks(dot(inputs_t[...], pre_back[:, columns]), out_a, out_b, pl.ds(0, cut))
        if out_a is sent_a:
            for i in range(max(ny, nz)):
                for ring in rings:
                    order = offsets(ring.count) + [0]
                    if i < ring.count:
                        ring.pair(order[i], other)

    def table_part():
        sums = dot(hot_rows(sender_row, table.shape[0]), pre_back[...]).astype(BF16)
        grads = dot_nt(sums, w_first[pl.ds(width, width)])
        local_grad[...] = grads[:nodes]
        halo_grad[...] = grads[nodes:].astype(BF16).reshape(4, slots, width)

    def receiver_part():
        sums = dot(hot_rows(receiver_row, nodes), pre_back[...]).astype(BF16)
        local_grad[...] += dot_nt(sums, w_first[pl.ds(2 * width, width)]) + cot[...].astype(F32)

    stores = []

    def store(src, dst):
        copy = pltpu.make_async_copy(src, dst, store_sems.at[len(stores)])
        copy.start()
        stores.append(copy)

    def edge_part():
        edge_grad_out[...] = (upstream[...] + dot_nt(pre_back[...], w_first[pl.ds(0, width)])).astype(BF16)
        store(edge_grad_out, edge_grad_hbm)

    work = [table_part, receiver_part, edge_part]
    for step in range(max(nz, ny) // 2):
        for ring in rings:
            ring.step(step)
        if work:
            work.pop(0)()
    for part in work:
        part()
    rings[0].finish(over_a, over_sent_a)
    rings[1].finish(over_b, over_sent_b)
    to_z = scatter(comm, "z", lambda peer: over_sent_a.at[peer], cross_a)
    to_y = scatter(comm, "y", lambda peer: over_sent_b.at[peer], cross_b)
    back_sem, back_group = comm.recv_sem(), comm.group(halo_grad)
    for k, to in enumerate(
        (wide_neighbour(-1), wide_neighbour(1), narrow_neighbour(-1), narrow_neighbour(1))
    ):
        comm.copy(back_group, halo_grad.at[k], returned.at[k], to, back_sem)
    share[0] = total_of(to_z, over_a[lax.axis_index("z")]).astype(BF16)
    share[1] = total_of(to_y, over_b[lax.axis_index("y")]).astype(BF16)
    here = lax.axis_index("x") * 2 + c
    shares[here] = share[...]
    group = comm.group(shares.at[pl.ds(0, 2 * across - 1)])
    copies = [comm.copy(group, share, shares.at[here], device) for device in narrow_peers()]
    for copy in copies:
        copy.wait_recv()
    slabs = []
    for core in (0, 1):
        for i in (0, 1):
            value = shares[core, i].astype(F32)
            for x in range(1, across):
                value = value + shares[2 * x + core, i].astype(F32)
            slabs.append(value)
    grads = jnp.concatenate(slabs, 1)
    square = grads * grads
    squares[0] = slab_rows(square[:cut], square[cut:])
    to_y = scatter(comm, "y", lambda peer: squares.at[0], squares_in.at[pl.ds(0, ny - 1)])
    squares[1] = total_of(to_y, squares[0])
    to_z = scatter(comm, "z", lambda peer: squares.at[1], squares_in.at[pl.ds(ny - 1, nz - 1)])
    wait_for(returned, back_sem)
    node_grad_out[...] = (
        local_grad[...] + dot(hot_rows(send_row, nodes), returned[...].reshape(4 * slots, width))
    ).astype(BF16)
    store(node_grad_out, node_grad_hbm)
    grad_sq = total_of(to_z, squares[1])
    factors = [clip_rows(grad_sq, weight_sq[...], which) for which in (0, 1)]
    for i in range(4):
        columns = slice(128 * i, 128 * (i + 1))
        first = factors[0][2 * i : 2 * i + 1] * math.sqrt(cut * nz * ny)
        second = factors[1][2 * i + 1 : 2 * i + 2] * math.sqrt(rest * nz * ny)
        first_out[:, columns] = grads[:cut, columns] * first
        second_out[:, columns] = grads[cut:, columns] * second
    store(first_out, first_hbm)
    store(second_out, second_hbm)
    comm.drain()
    for copy in stores:
        copy.wait()


def deliver(*refs):
    count = (len(refs) - 2) // 3
    moves = []
    for i in sorted(range(count), key=lambda i: -refs[i].shape[0]):
        source, target, held = refs[i], refs[count + i], refs[2 * count + i]
        height = min(128, source.shape[0])
        for j in range(source.shape[0] // height):
            rows, k = pl.ds(j * height, height), len(moves)
            load = pltpu.make_async_copy(source.at[rows], held.at[rows], refs[-2].at[k])
            load.start()
            moves.append((load, pltpu.make_async_copy(held.at[rows], target.at[rows], refs[-1].at[k])))
    for load, store in moves:
        load.wait()
        store.start()
    for _, store in moves:
        store.wait()


def per_device(
    node_latent,
    edge_latent,
    node_cotangent,
    w_first,
    bias_first,
    w_second,
    bias_second,
    norm_gain,
    send_map,
    edge_sender,
    edge_receiver,
):
    nz, ny, across = lax.axis_size("z"), lax.axis_size("y"), lax.axis_size("x")
    nodes, width = node_latent.shape
    edges = edge_latent.shape[0]
    slots = send_map.shape[2]
    table_rows = nodes + 4 * slots
    first_rows, second_rows = w_first.shape[0] // (nz * ny), w_second.shape[0] // (nz * ny)
    rows = first_rows + second_rows
    hbm = pl.BlockSpec(memory_space=pltpu.HBM)
    copies = 1 + 3 * (ny + nz) - 4 + 2 + 2 * across - 1 + 3
    results = pl.pallas_call(
        kernel,
        out_shape=(
            jax.ShapeDtypeStruct((nodes, width), BF16),
            jax.ShapeDtypeStruct((edges, width), BF16),
            jax.ShapeDtypeStruct((first_rows, width), F32),
            jax.ShapeDtypeStruct((second_rows, width), F32),
        ),
        in_specs=[hbm] * 11,
        out_specs=(hbm,) * 4,
        scratch_shapes=[
            pltpu.VMEM(send_map.shape, jnp.int32),
            pltpu.VMEM((edges,), jnp.int32),
            pltpu.VMEM((edges,), jnp.int32),
            pltpu.VMEM((width,), BF16),
            pltpu.VMEM((width,), BF16),
            pltpu.VMEM((width,), BF16),
            pltpu.VMEM((table_rows, width), BF16),
            pltpu.VMEM((edges, width), BF16),
            pltpu.VMEM((nodes, width), BF16),
            pltpu.VMEM((3 * width, width), BF16),
            pltpu.VMEM((width, width), BF16),
            pltpu.VMEM((4, slots, width), BF16),
            pltpu.VMEM((3 * width, edges), BF16),
            pltpu.VMEM((edges, width), F32),
            pltpu.VMEM((edges, width), F32),
            pltpu.VMEM((width, edges), BF16),
            pltpu.VMEM((edges, width), BF16),
            pltpu.VMEM((edges, width), BF16),
            pltpu.VMEM((edges, table_rows), BF16),
            pltpu.VMEM((edges, 1), F32),
            pltpu.VMEM((edges, width), BF16),
            pltpu.VMEM((8, 128), F32),
            pltpu.VMEM((4, slots, width), BF16),
            pltpu.VMEM((4, slots, width), BF16),
            pltpu.VMEM((nodes, width), F32),
            pltpu.VMEM((ny, nz, rows, 128), BF16),
            pltpu.VMEM((nz, ny, rows, 128), BF16),
            pltpu.VMEM((ny, nz, rows, 128), BF16),
            pltpu.VMEM((nz, ny, rows, 128), BF16),
            pltpu.VMEM((ny, nz, rows, 128), F32),
            pltpu.VMEM((nz, ny, rows, 128), F32),
            pltpu.VMEM((2 * (ny - 1), nz // 2, rows, 128), BF16),
            pltpu.VMEM((2 * (nz - 1), ny // 2, rows, 128), BF16),
            pltpu.VMEM((2 * (ny - 1), nz // 2, rows, 128), BF16),
            pltpu.VMEM((2 * (nz - 1), ny // 2, rows, 128), BF16),
            pltpu.VMEM((nz, rows, 128), F32),
            pltpu.VMEM((ny, rows, 128), F32),
            pltpu.VMEM((nz, rows, 128), BF16),
            pltpu.VMEM((ny, rows, 128), BF16),
            pltpu.VMEM((nz - 1, rows, 128), BF16),
            pltpu.VMEM((ny - 1, rows, 128), BF16),
            pltpu.VMEM((2, rows, 128), BF16),
            pltpu.VMEM((2 * across, 2, rows, 128), BF16),
            pltpu.VMEM((2, 8, 128), F32),
            pltpu.VMEM((ny - 1 + nz - 1, 8, 128), F32),
            pltpu.VMEM((nodes, width), BF16),
            pltpu.VMEM((edges, width), BF16),
            pltpu.VMEM((first_rows, width), F32),
            pltpu.VMEM((second_rows, width), F32),
            pltpu.SemaphoreType.DMA((11,)),
            pltpu.SemaphoreType.DMA((4,)),
            pltpu.SemaphoreType.DMA((11,)),
            pltpu.SemaphoreType.DMA((copies,)),
        ],
        compiler_params=pltpu.CompilerParams(
            collective_id=0, has_side_effects=True, vmem_limit_bytes=56 << 20
        ),
    )(
        send_map,
        edge_sender,
        edge_receiver,
        bias_first,
        bias_second,
        norm_gain,
        node_latent,
        edge_latent,
        node_cotangent,
        w_first,
        w_second,
    )
    return pl.pallas_call(
        deliver,
        out_shape=[jax.ShapeDtypeStruct(v.shape, v.dtype) for v in results],
        in_specs=[hbm] * 4,
        out_specs=[hbm] * 4,
        scratch_shapes=[pltpu.VMEM(v.shape, v.dtype) for v in results]
        + [pltpu.SemaphoreType.DMA((7,))] * 2,
        compiler_params=pltpu.CompilerParams(vmem_limit_bytes=56 << 20),
    )(*results)


def solution(mesh):
    finer = Mesh(mesh.devices.reshape(8, 8, 4, 2), ALL)
    in_specs = (
        P(ALL, None),
        P(ALL, None),
        P(ALL, None),
        P(),
        P(),
        P(),
        P(),
        P(),
        P(ALL, None, None),
        P(ALL),
        P(ALL),
    )
    out_specs = (P(ALL, None), P(ALL, None), P(WIDE, None), P(WIDE, None))
    return jax.shard_map(
        per_device, mesh=finer, in_specs=in_specs, out_specs=out_specs, check_vma=False
    )
```
